32 devices in a mesh: groups: 2 (over x), seq: 16 (over z, y, core).
Axes of the slice: x: 2, y: 2, z: 4, core: 2. Of those that a mesh axis runs over, the one named last changes fastest.
Arguments:
- query_rows: bfloat16 [8192, 1024], P(('groups', 'seq')), parts along dimension 0, may hold values from -25 to 25
- key_rows: bfloat16 [8192, 1024], P(('groups', 'seq')), parts along dimension 0, may hold values from -18 to 18
- value_rows: bfloat16 [8192, 1024], P(('groups', 'seq')), parts along dimension 0, may hold values from -18 to 18
- segment_ids: int32 [8192], P(('groups', 'seq')), parts along dimension 0, may hold values from 0 to 2, never falling along the last dimension, each value on 1 to 2560 neighbouring positions
- out_weight: bfloat16 [1024, 1024], replicated, may hold values from -0.1875 to 0.1875
Outputs:
- attended: bfloat16 [8192, 1024], P(('groups', 'seq')), parts along dimension 0
The draws below stay inside these ranges and needn't reach their ends.
There are 2 independent parts, one for each index of `groups`. The reference program is written for one: setup_inputs(seed, part) draws one part's arguments, and reference() takes and returns one part's arrays. A program takes and returns all parts, laid end to end along the dimension named above; an argument that names none is the same for every part. Nothing has to cross between parts.
Inputs may be any that keep to these rules, and one draw needn't show every extreme that they name: `segment_ids`: ids never fall along the sequence; there are three transcripts, one of exactly 2560 tokens.
All inputs are finite; a program needn't handle non-finite values.
Results may differ from the reference program's by a relative error of at most 0.0051.
Values may be sent and summed in bfloat16 or wider, within the bound.
A program may use at most 128 MiB of HBM per device.

```python
import math
import jax
import jax.numpy as jnp
import numpy as np
from jax import lax

H = 16
DH = 64
TILE = 128
TOK_DEV = 256
TOKENS = 4096
SHARD_BITS = 1
SEQ_BITS = 4
N_SEQ = 16


def smooth_rows(seed_key, amplitude):
    waves = jax.random.randint(jax.random.fold_in(seed_key, 1), (1, H * DH), 1, 5).astype(jnp.float32)
    offsets = jax.random.uniform(jax.random.fold_in(seed_key, 2), (1, H * DH), dtype=jnp.float32, minval=0.0, maxval=2.0 * math.pi)
    positions = jnp.arange(TOKENS).astype(jnp.float32)[:, None]
    return amplitude * jnp.sin(2.0 * math.pi * waves * positions / TOKENS + offsets)


def block_offsets(seed_key):
    width = H * DH
    total = jnp.zeros((TOKENS, width), dtype=jnp.float32)
    scale_count = (TOKENS // (2 * TILE)).bit_length() - 1
    for level in range(1, scale_count + 1):
        span = 2 ** level
        table = jax.random.uniform(jax.random.fold_in(seed_key, level), (TOKENS // span, 1, width), dtype=jnp.float32, minval=-0.6, maxval=0.6)
        total = (total.reshape(TOKENS // span, span, width) + table).reshape(TOKENS, width)
    return total


def rough_rows(seed_key):
    jitter = jnp.clip(jax.random.normal(jax.random.fold_in(seed_key, 1), (TOKENS, H * DH), dtype=jnp.float32), -5.0, 5.0)
    scales = jnp.exp(jax.random.uniform(jax.random.fold_in(seed_key, 2), (TOKENS, 1), dtype=jnp.float32, minval=math.log(0.3), maxval=math.log(3.0)))
    return jitter * scales


def key_field(seed_key):
    folded = jax.random.fold_in(seed_key, 101)
    surface = rough_rows(jax.random.fold_in(folded, 1)) + smooth_rows(jax.random.fold_in(folded, 2), 1.5) + block_offsets(jax.random.fold_in(folded, 3))
    surface = jnp.clip(surface, -18.0, 18.0)
    return surface


def draw_key_rows(key, part):
    return key_field(key).astype(jnp.bfloat16)


def draw_value_rows(key, part):
    folded = jax.random.fold_in(key, 404)
    surface = rough_rows(jax.random.fold_in(folded, 1)) + smooth_rows(jax.random.fold_in(folded, 2), 2.0) + block_offsets(jax.random.fold_in(folded, 3))
    return jnp.clip(surface, -18.0, 18.0).astype(jnp.bfloat16)


def draw_query_rows(key, part):
    folded = jax.random.fold_in(key, 505)
    jitter = jnp.clip(jax.random.normal(folded, (TOKENS, H * DH), dtype=jnp.float32), -5.0, 5.0)
    return jitter.astype(jnp.bfloat16)


def profile(count, total, most, lean):
    portions = [(1 << 20) // math.isqrt(rank ** lean) + 1 for rank in range(2, count + 1)]
    spare, given = total - most - (count - 1), [1] * (count - 1)
    while spare > 0:
        candidates = [i for i in range(count - 1) if given[i] < most]
        mass, left = sum([portions[i] for i in candidates]), spare
        for i in candidates:
            more = min(most - given[i], max(1, left * portions[i] // mass), spare)
            given[i] = given[i] + more
            spare = spare - more
    return np.array([most] + given)


def uneven(key, number_of, total, limit, lean):
    if number_of == 2:
        one = jax.random.randint(key, (), max(1, total - limit), min(limit, total - 1) + 1)
        return jnp.stack([one, total - one])
    tallies = jnp.asarray(profile(number_of, total, limit, lean), jnp.int32)
    twos = (number_of - 1) // 2
    donor, receiver = tallies[1:1 + 2 * twos:2], tallies[2:2 + 2 * twos:2]
    room = jnp.minimum(donor - 1, limit - receiver)
    moved = jax.random.randint(jax.random.fold_in(key, 1), (twos,), 0, 1 << 20) % (room + 1)
    tallies = tallies.at[1:1 + 2 * twos:2].set(donor - moved).at[2:2 + 2 * twos:2].set(receiver + moved)
    return tallies[jax.random.permutation(jax.random.fold_in(key, 2), number_of)]


def bell_draw(stream_key, extent, spread, most, kind=jnp.bfloat16):
    array = spread * jax.random.normal(stream_key, extent, jnp.float32)
    return jnp.clip(array, min=-most, max=most).astype(kind)


def setup_inputs(seed: int = 0, part: int = 0) -> dict:
    key_of = jax.random.split(jax.random.key(seed), 6)
    part_splits = jax.random.split(jax.random.fold_in(key_of[5], part), 6)
    query_rows = draw_query_rows(jax.random.fold_in(jax.random.fold_in(key_of[5], part), 71), part)
    key_rows = draw_key_rows(jax.random.fold_in(jax.random.fold_in(key_of[5], part), 71), part)
    value_rows = draw_value_rows(jax.random.fold_in(jax.random.fold_in(key_of[5], part), 71), part)
    segment_ids = jnp.searchsorted(jnp.cumsum(uneven(part_splits[3], 3, TOKENS, 5 * TOKENS // 8, 2)), jnp.arange(TOKENS), side="right").astype(jnp.int32)
    out_weight = bell_draw(key_of[4], (H * DH, H * DH), (H * DH) ** -0.5, 0.1875)
    return dict(query_rows=query_rows, key_rows=key_rows, value_rows=value_rows, segment_ids=segment_ids, out_weight=out_weight)


def level_terms(query_blocks, key_blocks, value_blocks, allowed):
    scores = jnp.einsum('gmhd,gkhd->ghmk', query_blocks.astype(jnp.float32), key_blocks.astype(jnp.float32)) * (DH ** -0.5)
    key_mask = allowed[:, None, :, :]
    largest = jnp.max(jnp.where(key_mask, scores, -1e30), axis=-1)
    weights = jnp.exp(jnp.where(key_mask, scores - largest[..., None], -1e30))
    totals = jnp.sum(weights, axis=-1)
    rounded = weights.astype(jnp.bfloat16)
    weighted = jnp.einsum('ghmk,gkhd->gmhd', rounded.astype(jnp.float32), value_blocks.astype(jnp.float32))
    groups = query_blocks.shape[0]
    members = query_blocks.shape[1]
    largest = jnp.transpose(largest, (0, 2, 1)).reshape(groups * members, H)
    totals = jnp.transpose(totals, (0, 2, 1)).reshape(groups * members, H)
    return largest, totals, weighted.reshape(groups * members, H, DH)


def merge_terms(running, terms):
    new_max = jnp.maximum(running[0], terms[0])
    keep_old = jnp.exp(running[0] - new_max)
    keep_new = jnp.exp(terms[0] - new_max)
    totals = running[1] * keep_old + terms[1] * keep_new
    weighted = running[2] * keep_old[..., None] + terms[2] * keep_new[..., None]
    return new_max, totals, weighted


def pair_mean(source_rows):
    paired = source_rows.reshape(source_rows.shape[0] // 2, 2, source_rows.shape[1]).astype(jnp.float32)
    return ((paired[:, 0] + paired[:, 1]) * 0.5).astype(jnp.bfloat16)


def reference(query_rows, key_rows, value_rows, segment_ids, out_weight):
    width = H * DH
    levels = SHARD_BITS + SEQ_BITS
    seg_plus = segment_ids + 1
    coarse = []
    prev_keys = key_rows
    prev_values = value_rows
    for level_index in range(1, levels):
        factor = 2 ** level_index
        prev_keys = pair_mean(prev_keys)
        prev_values = pair_mean(prev_values)
        seg_pairs = seg_plus.reshape(TOKENS // factor, factor)
        coarse.append((prev_keys, prev_values, seg_pairs[:, 0], seg_pairs[:, factor - 1]))
    key_pad = jnp.pad(key_rows, ((TILE, TILE), (0, 0)))
    value_pad = jnp.pad(value_rows, ((TILE, TILE), (0, 0)))
    seg_pad = jnp.pad(seg_plus, (TILE, TILE))
    tile_count = TOK_DEV // TILE

    def one_shard(shard_index):
        first_row = shard_index * TOK_DEV
        query_shard = lax.dynamic_slice_in_dim(query_rows, first_row, TOK_DEV, 0).reshape(TOK_DEV, H, DH)
        seg_shard = lax.dynamic_slice_in_dim(seg_plus, first_row, TOK_DEV, 0)
        key_span = lax.dynamic_slice_in_dim(key_pad, first_row, TOK_DEV + 2 * TILE, 0).reshape(tile_count + 2, TILE, H, DH)
        value_span = lax.dynamic_slice_in_dim(value_pad, first_row, TOK_DEV + 2 * TILE, 0).reshape(tile_count + 2, TILE, H, DH)
        seg_span = lax.dynamic_slice_in_dim(seg_pad, first_row, TOK_DEV + 2 * TILE, 0).reshape(tile_count + 2, TILE)
        key_window = jnp.concatenate([key_span[:-2], key_span[1:-1], key_span[2:]], axis=1)
        value_window = jnp.concatenate([value_span[:-2], value_span[1:-1], value_span[2:]], axis=1)
        seg_window = jnp.concatenate([seg_span[:-2], seg_span[1:-1], seg_span[2:]], axis=1)
        seg_tiles = seg_shard.reshape(tile_count, TILE)
        allowed = seg_tiles[:, :, None] == seg_window[:, None, :]
        running = level_terms(query_shard.reshape(tile_count, TILE, H, DH), key_window, value_window, allowed)
        for level_index in range(1, levels):
            block_size = TILE * 2 ** level_index
            coarse_keys, coarse_values, seg_first, seg_last = coarse[level_index - 1]
            if 2 * block_size <= TOK_DEV:
                groups = TOK_DEV // block_size
                start_row = first_row // (2 ** level_index)
                row_count = groups * TILE

                def sibling(array_in):
                    taken = lax.dynamic_slice_in_dim(array_in, start_row, row_count, 0)
                    shaped = taken.reshape((groups // 2, 2, TILE) + array_in.shape[1:])
                    return shaped[:, ::-1].reshape((groups, TILE) + array_in.shape[1:])

                key_blocks = sibling(coarse_keys).reshape(groups, TILE, H, DH)
                value_blocks = sibling(coarse_values).reshape(groups, TILE, H, DH)
                first_blocks = sibling(seg_first)
                last_blocks = sibling(seg_last)
                query_blocks = query_shard.reshape(groups, block_size, H, DH)
                seg_blocks = seg_shard.reshape(groups, block_size)
            else:
                block_index = first_row // block_size
                start_row = jnp.bitwise_xor(block_index, 1) * TILE
                key_blocks = lax.dynamic_slice_in_dim(coarse_keys, start_row, TILE, 0).reshape(1, TILE, H, DH)
                value_blocks = lax.dynamic_slice_in_dim(coarse_values, start_row, TILE, 0).reshape(1, TILE, H, DH)
                first_blocks = lax.dynamic_slice_in_dim(seg_first, start_row, TILE, 0)[None]
                last_blocks = lax.dynamic_slice_in_dim(seg_last, start_row, TILE, 0)[None]
                query_blocks = query_shard[None]
                seg_blocks = seg_shard[None]
            allowed = (seg_blocks[:, :, None] == first_blocks[:, None, :]) & (seg_blocks[:, :, None] == last_blocks[:, None, :])
            running = merge_terms(running, level_terms(query_blocks, key_blocks, value_blocks, allowed))
        context = (running[2] / running[1][..., None]).astype(jnp.bfloat16).reshape(TOK_DEV, width)
        return jnp.dot(context, out_weight, preferred_element_type=jnp.float32).astype(jnp.bfloat16)

    result = lax.map(one_shard, jnp.arange(N_SEQ, dtype=jnp.int32))
    return result.reshape(TOKENS, width)
```

```python
import functools
import jax
import jax.numpy as jnp
from jax import lax
from jax.experimental import pallas as pl
from jax.experimental.pallas import tpu as pltpu
from jax.sharding import PartitionSpec as P

DH = 64
TILE = 128
LANES = 128
HALF = 64
BIG = 2.0**100
MESH = pl.DeviceIdType.MESH


def flip(index, mask):
    bit = 0
    while (1 << bit) <= mask:
        if mask & (1 << bit):
            index = index + (1 - 2 * ((index // (1 << bit)) % 2)) * (1 << bit)
        bit += 1
    return index


def halve(source):
    rows = source.shape[0]
    row = lax.broadcasted_iota(jnp.int32, (rows // 2, rows), 0)
    col = lax.broadcasted_iota(jnp.int32, (rows // 2, rows), 1)
    pick = jnp.where(col // 2 == row, 0.5, 0.0).astype(jnp.bfloat16)
    return jnp.dot(pick, source, preferred_element_type=jnp.float32).astype(jnp.bfloat16)


def attend(devices, q_hbm, k_hbm, v_hbm, seg_hbm, w_hbm, out_ref, q_ref, seg_ref, load_sem, kv, coarse, inner, cross,
           queries, query_seg, largest, total, context, w_vmem, w_sem, send_sem, recv_sem, *rest):
    levels = devices.bit_length() - 1
    sends = dict(zip(range(2, levels + 1), rest))
    blocks = dict(zip(range(1, levels + 1), rest[levels - 1 :]))
    me = lax.axis_index("seq")
    core = me % 2
    tokens, width = q_hbm.shape
    pairs = width // LANES
    part = width // 2
    seg_at = 2 * part
    parts = (slice(0, 2 * part + LANES), slice(2 * part + LANES, 4 * part + LANES))
    every = slice(0, 4 * part + LANES)
    seg_columns = slice(seg_at, seg_at + LANES)

    middle = (me // 4 + me // 8) % 2 == 1
    outer = jnp.logical_not(middle)
    has_cross = jnp.logical_and(me + core > 0, me + core < devices)
    neighbour = me - 1 + 2 * core
    inner_row = pl.multiple_of((1 - core) * TILE, TILE)
    cross_row = pl.multiple_of(core * TILE, TILE)
    mine = pl.multiple_of(core * HALF, HALF)

    barrier = pltpu.get_barrier_semaphore()
    masks = [1, 2, 4] + [1 << (level - 1) for level in range(5, levels + 1)]
    for mask in masks:
        pl.semaphore_signal(barrier, inc=1, device_id={"seq": flip(me, mask)}, device_id_type=MESH)

    @pl.when(middle)
    def _():
        pl.semaphore_signal(barrier, inc=1, device_id={"seq": flip(me, 12)}, device_id_type=MESH)

    @pl.when(has_cross)
    def _():
        pl.semaphore_signal(barrier, inc=1, device_id={"seq": neighbour}, device_id_type=MESH)

    def load(source, index, from_cols, to_cols):
        return pltpu.make_async_copy(source.at[:, from_cols], kv.at[:, to_cols], load_sem.at[index])

    seg_load = pltpu.make_async_copy(seg_hbm, seg_ref, load_sem.at[0])
    q_load = pltpu.make_async_copy(q_hbm, q_ref, load_sem.at[1])
    loads = []
    for h in range(2):
        base = parts[h].start
        loads.append([
            load(k_hbm, 2 + 2 * h, slice(h * part, (h + 1) * part), slice(base, base + part)),
            load(v_hbm, 3 + 2 * h, slice(h * part, (h + 1) * part),
                 slice(base + part, base + 2 * part)),
        ])
    seg_load.start()
    for some in loads:
        for one_load in some:
            one_load.start()
    q_load.start()
    seg_load.wait()

    seg = seg_ref[...]
    first = jnp.sum(jnp.where(seg < 1, 1.0, 0.0), axis=1, keepdims=True)
    second = jnp.sum(jnp.where(seg < 2, 1.0, 0.0), axis=1, keepdims=True)
    row = lax.broadcasted_iota(jnp.int32, (tokens, LANES), 0).astype(jnp.float32)
    lane = lax.broadcasted_iota(jnp.int32, (tokens, LANES), 1).astype(jnp.float32)
    row_seg = jnp.where(row >= first, 1.0, 0.0) + jnp.where(row >= second, 1.0, 0.0)
    kv[:, seg_columns] = jnp.where(lane == row_seg, -BIG, 0.0).astype(jnp.bfloat16)
    other = jnp.where(lane == row_seg, 0.0, jnp.where(lane < 4, 1.0, 0.0)).astype(jnp.bfloat16)
    query_seg[:tokens, :] = other
    query_seg[tokens:, :] = other

    @pl.when(jnp.logical_not(has_cross))
    def _():
        cross[...] = jnp.zeros(cross.shape, cross.dtype)
        spot = lax.broadcasted_iota(jnp.int32, (TILE, LANES), 1)
        cross[:, seg_columns] = jnp.where(spot == 3, -BIG, 0.0).astype(jnp.bfloat16)

    made = []

    def remote(source, target, device):
        index = len(made)
        copy = pltpu.make_async_remote_copy(
            src_ref=source, dst_ref=target, send_sem=send_sem.at[index],
            recv_sem=recv_sem.at[index], device_id={"seq": device}, device_id_type=MESH)
        made.append(copy)
        return copy

    def block_part(level, start, rows, cols):
        return blocks[level].at[pl.ds(pl.multiple_of(mine + start, 16), rows), cols]

    def exchange(level, start, rows, cols, mask):
        return remote(sends[level].at[start : start + rows, cols],
                      block_part(level, start, rows, cols), flip(me, mask))

    def forward(level, start, rows, cols, mask=1):
        here = block_part(level, start, rows, cols)
        return remote(here, here, flip(me, mask))

    to_sibling = remote(coarse, blocks[1], flip(me, 1))
    to_inner = remote(kv.at[pl.ds(inner_row, TILE)], inner, flip(me, 1))
    to_cross = [remote(kv.at[pl.ds(cross_row, TILE), cols], cross.at[:, cols], neighbour)
                for cols in parts]
    second_out = [exchange(2, 0, HALF, cols, 2) for cols in parts]
    second_on = [forward(2, 0, HALF, cols) for cols in parts]
    third_early = exchange(3, 0, 32, every, 4)
    third_early_on = forward(3, 0, 32, every)
    third_out = [exchange(3, 32, 32, cols, 4) for cols in parts]
    third_on = [forward(3, 32, 32, cols) for cols in parts]
    pieces = [(start, cols) for start in (0, 32) for cols in parts]
    fourth_out = [exchange(4, start, 32, cols, 12) for start, cols in pieces]
    fourth_on = [forward(4, start, 32, cols) for start, cols in pieces]
    fourth_away = [forward(4, start, 32, cols, 4) for start, cols in pieces]
    later_out = {level: exchange(level, 0, HALF, every, 1 << (level - 1))
                 for level in range(5, levels + 1)}
    later_on = {level: forward(level, 0, HALF, every) for level in range(5, levels + 1)}

    def when_start(condition, copy):
        pl.when(condition)(copy.start)

    for h, cols in enumerate(parts):
        for one_load in loads[h]:
            one_load.wait()
        coarse[:, cols] = halve(kv[:, cols])
        sends[2][:, cols] = halve(coarse[:, cols])
        if h == 0:
            pl.semaphore_wait(barrier, len(masks) + jnp.where(middle, 1, 0) + jnp.where(has_cross, 1, 0))
        second_out[h].start()
    to_sibling.start()
    to_inner.start()
    sends[3][:32, :] = halve(sends[2][...])
    third_early.start()
    sends[4][:16, :] = halve(sends[3][:32, :])
    for copy in to_cross:
        when_start(has_cross, copy)
    w_copy = pltpu.make_async_copy(w_hbm, w_vmem, w_sem)
    w_copy.start()
    q_load.wait()

    low_lanes = lax.broadcasted_iota(jnp.int32, (TILE, LANES), 1) < DH
    one = jnp.ones((TILE, LANES), jnp.bfloat16)
    zero = jnp.zeros((TILE, LANES), jnp.bfloat16)
    low_ones = jnp.where(low_lanes, one, zero)
    high_ones = jnp.where(low_lanes, zero, one)

    def columns(h, pair):
        at = parts[h].start + (pair - h * (pairs // 2)) * LANES
        return (pl.ds(pl.multiple_of(at, LANES), LANES),
                pl.ds(pl.multiple_of(at + part, LANES), LANES))

    def score(left_side, spots, key_cols):
        right_side = jnp.concatenate(
            [jnp.concatenate([ref[base : base + TILE, key_cols], ref[base : base + TILE, seg_columns]],
                             axis=1) for ref, base in spots], axis=0)
        return lax.dot_general(left_side, right_side, (((1,), (1,)), ((), ())),
                               preferred_element_type=jnp.float32)

    def highest(scores):
        top = scores[:, :LANES]
        for at in range(LANES, scores.shape[1], LANES):
            top = jnp.maximum(top, scores[:, at : at + LANES])
        return jnp.broadcast_to(jnp.max(top, axis=1, keepdims=True), top.shape)

    def weigh(scores, top, spots, value_cols):
        half = top.shape[0] // 2
        left_side, right_side = [], []
        for index, (ref, base) in enumerate(spots):
            some = scores[:, index * LANES : (index + 1) * LANES]
            weights = jnp.exp(some - top).astype(jnp.bfloat16)
            values = ref[base : base + TILE, value_cols]
            left_side += [weights[:half], weights[half:]]
            right_side += [
                jnp.concatenate([jnp.where(low_lanes, values, zero), low_ones], axis=1),
                jnp.concatenate([jnp.where(low_lanes, zero, values), high_ones], axis=1),
            ]
        return jnp.dot(jnp.concatenate(left_side, axis=1), jnp.concatenate(right_side, axis=0),
                       preferred_element_type=jnp.float32)

    def rescale(old, top):
        shrink = jnp.exp(old - top)
        half = top.shape[0] // 2
        lanes = lax.broadcasted_iota(jnp.int32, (half, LANES), 1) < DH
        both = jnp.where(lanes, shrink[:half], shrink[half:])
        return jnp.concatenate([both, both], axis=1)

    def whole_step(h, pair, spots):
        key_cols, value_cols = columns(h, pair)
        left_side = jnp.concatenate([queries[pair], query_seg[...]], axis=1)
        scores = score(left_side, spots, key_cols)
        old = largest[pair]
        top = jnp.maximum(old, highest(scores))
        largest[pair] = top
        total[pair] = total[pair] * rescale(old, top) + weigh(scores, top, spots, value_cols)

    def tile_step(h, pair, start, spots, last):
        key_cols, value_cols = columns(h, pair)
        heads = (pl.ds(start, TILE), pl.ds(pl.multiple_of(start + tokens, TILE), TILE))
        left_side = jnp.concatenate(
            [jnp.concatenate([queries[pair, head], query_seg[head, :]], axis=1) for head in heads], axis=0)
        scores = score(left_side, spots, key_cols)
        old = jnp.concatenate([largest[pair, head] for head in heads], axis=0)
        top = jnp.maximum(old, highest(scores))
        acc = total[pair, heads[0]] * rescale(old, top) + weigh(scores, top, spots, value_cols)
        if last:
            context[heads[0], pl.ds(pl.multiple_of(pair * LANES, LANES), LANES)] = (
                acc[:, :LANES] / acc[:, LANES:]).astype(jnp.bfloat16)
        else:
            for index, head in enumerate(heads):
                largest[pair, head] = top[index * TILE : (index + 1) * TILE]
            total[pair, heads[0]] = acc

    def halves(body):
        for h in range(2):
            pl.loop(h * (pairs // 2), (h + 1) * (pairs // 2), unroll=4)(functools.partial(body, h))

    near = [(kv, 0), (kv, TILE), (blocks[1], 0)]

    def first_step(h, pair):
        key_cols, value_cols = columns(h, pair)
        scaled = q_ref[:, pl.ds(pl.multiple_of(pair * LANES, LANES), LANES)] * jnp.bfloat16(DH**-0.5)
        lanes = lax.broadcasted_iota(jnp.int32, (tokens, LANES), 1) < DH
        none = jnp.zeros_like(scaled)
        both = jnp.concatenate([jnp.where(lanes, scaled, none), jnp.where(lanes, none, scaled)], axis=0)
        queries[pair] = both
        scores = score(jnp.concatenate([both, query_seg[...]], axis=1), near, key_cols)
        top = highest(scores)
        largest[pair] = top
        total[pair] = weigh(scores, top, near, value_cols)

    to_sibling.wait_recv()
    for h, cols in enumerate(parts):
        pl.loop(h * (pairs // 2), (h + 1) * (pairs // 2), unroll=4)(functools.partial(first_step, h))
        second_out[h].wait_recv()
        second_on[h].start()
        sends[3][32:, cols] = halve(blocks[2][pl.ds(mine, HALF), cols])
        third_out[h].start()
        sends[4][16:32, cols] = halve(sends[3][32:, cols])
        when_start(middle, fourth_out[h])

    to_inner.wait_recv()
    halves(lambda h, pair: tile_step(h, pair, inner_row, [(inner, 0)], False))

    third_early.wait_recv()
    third_early_on.start()
    for h, cols in enumerate(parts):
        third_out[h].wait_recv()
        third_on[h].start()
        sends[4][32:, cols] = halve(blocks[3][pl.ds(mine, HALF), cols])
        when_start(middle, fourth_out[2 + h])

    for copy in second_on + [third_early_on] + third_on:
        copy.wait_recv()
    halves(lambda h, pair: whole_step(h, pair, [(blocks[2], 0), (blocks[3], 0)]))

    @pl.when(middle)
    def _():
        for index in range(4):
            fourth_out[index].wait_recv()
            fourth_away[index].start()
            fourth_on[index].start()

    @pl.when(outer)
    def _():
        for index in range(4):
            fourth_away[index].wait_recv()
            fourth_on[index].start()

    for level in range(5, levels + 1):
        sends[level][:32, :] = halve(sends[level - 1][...])
        sends[level][32:, :] = halve(blocks[level - 1][pl.ds(mine, HALF), :])
        later_out[level].start()
        later_out[level].wait_recv()
        later_on[level].start()

    for copy in fourth_on + list(later_on.values()):
        copy.wait_recv()
    far = [(blocks[level], 0) for level in range(4, levels + 1)]
    halves(lambda h, pair: tile_step(h, pair, inner_row, far, True))

    @pl.when(has_cross)
    def _():
        for copy in to_cross:
            copy.wait_recv()

    halves(lambda h, pair: tile_step(h, pair, cross_row, far + [(cross, 0)], True))

    w_copy.wait()

    @pl.loop(0, out_ref.shape[1] // 256, unroll=4)
    def _(block):
        cols = pl.ds(pl.multiple_of(block * 256, 256), 256)
        out_ref[:, cols] = jnp.dot(context[...], w_vmem[:, cols],
                                   preferred_element_type=jnp.float32).astype(jnp.bfloat16)

    for copy in [to_sibling, to_inner, third_early, third_early_on] + second_out + second_on + third_out + third_on:
        copy.wait_send()
    for copy in fourth_on + list(later_out.values()) + list(later_on.values()):
        copy.wait_send()

    @pl.when(middle)
    def _():
        for copy in fourth_out + fourth_away:
            copy.wait_send()

    @pl.when(has_cross)
    def _():
        for copy in to_cross:
            copy.wait_send()


def on_device(devices, query_rows, key_rows, value_rows, segment_ids, out_weight):
    tokens, width = query_rows.shape
    levels = devices.bit_length() - 1
    span = 2 * width + LANES
    copies = 26 + 2 * (levels - 4)
    pairs = width // LANES
    bf16 = jnp.bfloat16
    scratch = [
        pltpu.VMEM((tokens, width), bf16),
        pltpu.VMEM((1, tokens), jnp.int32),
        pltpu.SemaphoreType.DMA((6,)),
        pltpu.VMEM((tokens, span), bf16),
        pltpu.VMEM((TILE, span), bf16),
        pltpu.VMEM((TILE, span), bf16),
        pltpu.VMEM((TILE, span), bf16),
        pltpu.VMEM((pairs, 2 * tokens, LANES), bf16),
        pltpu.VMEM((2 * tokens, LANES), bf16),
        pltpu.VMEM((pairs, 2 * tokens, LANES), jnp.float32),
        pltpu.VMEM((pairs, tokens, 2 * LANES), jnp.float32),
        pltpu.VMEM((tokens, width), bf16),
        pltpu.VMEM(out_weight.shape, bf16),
        pltpu.SemaphoreType.DMA,
        pltpu.SemaphoreType.DMA((copies,)),
        pltpu.SemaphoreType.DMA((copies,)),
    ]
    scratch += [pltpu.VMEM((HALF, span), bf16) for _ in range(2, levels + 1)]
    scratch += [pltpu.VMEM((TILE, span), bf16) for _ in range(1, levels + 1)]
    vmem = pl.BlockSpec(memory_space=pltpu.VMEM)
    return pl.pallas_call(
        functools.partial(attend, devices),
        out_shape=jax.ShapeDtypeStruct((tokens, width), bf16),
        in_specs=[pl.BlockSpec(memory_space=pltpu.HBM)] * 5,
        out_specs=vmem,
        scratch_shapes=scratch,
        compiler_params=pltpu.CompilerParams(
            collective_id=0, has_side_effects=True),
    )(query_rows, key_rows, value_rows, segment_ids.reshape(1, tokens), out_weight)


def solution(mesh):
    rows = P(("groups", "seq"), None)
    return jax.shard_map(
        functools.partial(on_device, mesh.shape["seq"]), mesh=mesh,
        in_specs=(rows, rows, rows, P(("groups", "seq")), P()),
        out_specs=rows, check_vma=False)
```

```python
import functools
import jax
import jax.numpy as jnp
from jax import lax
from jax.experimental import pallas as pl
from jax.experimental.pallas import tpu as pltpu
from jax.sharding import PartitionSpec as P

DH = 64
TILE = 128
LANES = 128
HALF = 64
BIG = 2.0**100
MESH = pl.DeviceIdType.MESH


def flip(index, mask):
    bit = 0
    while (1 << bit) <= mask:
        if mask & (1 << bit):
            index = index + (1 - 2 * ((index // (1 << bit)) % 2)) * (1 << bit)
        bit += 1
    return index


def halve(source):
    rows = source.shape[0]
    row = lax.broadcasted_iota(jnp.int32, (rows // 2, rows), 0)
    col = lax.broadcasted_iota(jnp.int32, (rows // 2, rows), 1)
    pick = jnp.where(col // 2 == row, 0.5, 0.0).astype(jnp.bfloat16)
    return jnp.dot(pick, source, preferred_element_type=jnp.float32).astype(jnp.bfloat16)


def attend(devices, q_hbm, k_hbm, v_hbm, seg_hbm, w_hbm, out_ref, q_ref, seg_ref, load_sem, kv, coarse, inner, cross,
           queries, query_seg, largest, total, context, w_vmem, w_sem, send_sem, recv_sem, *rest):
    levels = devices.bit_length() - 1
    sends = dict(zip(range(2, levels + 1), rest))
    blocks = dict(zip(range(1, levels + 1), rest[levels - 1 :]))
    me = lax.axis_index("seq")
    core = me % 2
    tokens, width = q_hbm.shape
    pairs = width // LANES
    part = width // 2
    seg_at = 2 * part
    parts = (slice(0, 2 * part + LANES), slice(2 * part + LANES, 4 * part + LANES))
    every = slice(0, 4 * part + LANES)
    seg_columns = slice(seg_at, seg_at + LANES)

    middle = (me // 4 + me // 8) % 2 == 1
    outer = jnp.logical_not(middle)
    straight = (me // 2 + me // 4) % 2 == 0
    corner = jnp.logical_and(outer, straight)
    side = jnp.logical_and(outer, jnp.logical_not(straight))
    to_side = jnp.logical_and(middle, straight)
    has_cross = jnp.logical_and(me + core > 0, me + core < devices)
    neighbour = me - 1 + 2 * core
    inner_row = pl.multiple_of((1 - core) * TILE, TILE)
    cross_row = pl.multiple_of(core * TILE, TILE)
    mine = pl.multiple_of(core * HALF, HALF)

    barrier = pltpu.get_barrier_semaphore()
    masks = [1, 2, 4] + [1 << (level - 1) for level in range(5, levels + 1)]
    for mask in masks:
        pl.semaphore_signal(barrier, inc=1, device_id={"seq": flip(me, mask)}, device_id_type=MESH)

    @pl.when(middle)
    def _():
        pl.semaphore_signal(barrier, inc=1, device_id={"seq": flip(me, 12)}, device_id_type=MESH)

    @pl.when(has_cross)
    def _():
        pl.semaphore_signal(barrier, inc=1, device_id={"seq": neighbour}, device_id_type=MESH)

    def load(source, index, from_cols, to_cols):
        return pltpu.make_async_copy(source.at[:, from_cols], kv.at[:, to_cols], load_sem.at[index])

    seg_load = pltpu.make_async_copy(seg_hbm, seg_ref, load_sem.at[0])
    q_load = pltpu.make_async_copy(q_hbm, q_ref, load_sem.at[1])
    loads = []
    for h in range(2):
        base = parts[h].start
        loads.append([
            load(k_hbm, 2 + 2 * h, slice(h * part, (h + 1) * part), slice(base, base + part)),
            load(v_hbm, 3 + 2 * h, slice(h * part, (h + 1) * part),
                 slice(base + part, base + 2 * part)),
        ])
    seg_load.start()
    for some in loads:
        for one_load in some:
            one_load.start()
    q_load.start()
    seg_load.wait()

    seg = seg_ref[...]
    first = jnp.sum(jnp.where(seg < 1, 1.0, 0.0), axis=1, keepdims=True)
    second = jnp.sum(jnp.where(seg < 2, 1.0, 0.0), axis=1, keepdims=True)
    row = lax.broadcasted_iota(jnp.int32, (tokens, LANES), 0).astype(jnp.float32)
    lane = lax.broadcasted_iota(jnp.int32, (tokens, LANES), 1).astype(jnp.float32)
    row_seg = jnp.where(row >= first, 1.0, 0.0) + jnp.where(row >= second, 1.0, 0.0)
    kv[:, seg_columns] = jnp.where(lane == row_seg, -BIG, 0.0).astype(jnp.bfloat16)
    other = jnp.where(lane == row_seg, 0.0, jnp.where(lane < 4, 1.0, 0.0)).astype(jnp.bfloat16)
    query_seg[:tokens, :] = other
    query_seg[tokens:, :] = other

    @pl.when(jnp.logical_not(has_cross))
    def _():
        cross[...] = jnp.zeros(cross.shape, cross.dtype)
        spot = lax.broadcasted_iota(jnp.int32, (TILE, LANES), 1)
        cross[:, seg_columns] = jnp.where(spot == 3, -BIG, 0.0).astype(jnp.bfloat16)

    made = []

    def remote(source, target, device):
        index = len(made)
        copy = pltpu.make_async_remote_copy(
            src_ref=source, dst_ref=target, send_sem=send_sem.at[index],
            recv_sem=recv_sem.at[index], device_id={"seq": device}, device_id_type=MESH)
        made.append(copy)
        return copy

    def block_part(level, start, rows, cols):
        return blocks[level].at[pl.ds(pl.multiple_of(mine + start, 16), rows), cols]

    def exchange(level, start, rows, cols, mask):
        return remote(sends[level].at[start : start + rows, cols],
                      block_part(level, start, rows, cols), flip(me, mask))

    def forward(level, start, rows, cols, mask=1):
        here = block_part(level, start, rows, cols)
        return remote(here, here, flip(me, mask))

    to_sibling = remote(coarse, blocks[1], flip(me, 1))
    to_inner = remote(kv.at[pl.ds(inner_row, TILE)], inner, flip(me, 1))
    to_cross = [remote(kv.at[pl.ds(cross_row, TILE), cols], cross.at[:, cols], neighbour)
                for cols in parts]
    second_out = [exchange(2, 0, HALF, cols, 2) for cols in parts]
    second_on = [forward(2, 0, HALF, cols) for cols in parts]
    third_early = exchange(3, 0, 32, every, 4)
    third_early_on = forward(3, 0, 32, every)
    third_out = [exchange(3, 32, 32, cols, 4) for cols in parts]
    third_on = [forward(3, 32, 32, cols) for cols in parts]
    pieces = [(0, every), (32, every), (16, parts[0]), (16, parts[1]), (48, parts[0]), (48, parts[1])]
    fourth_out = [exchange(4, start, 16, cols, 12) for start, cols in pieces]
    fourth_on = [forward(4, start, 16, cols) for start, cols in pieces]
    fourth_away = [forward(4, start, 16, cols, 4) for start, cols in pieces]
    fourth_over = [remote(block_part(4, start, 16, every), block_part(4, start + 16, 16, every), flip(me, 2))
                   for start in (0, 32)]
    later_out = {level: exchange(level, 0, HALF, every, 1 << (level - 1))
                 for level in range(5, levels + 1)}
    later_on = {level: forward(level, 0, HALF, every) for level in range(5, levels + 1)}

    def when_start(condition, copy):
        pl.when(condition)(copy.start)

    for h, cols in enumerate(parts):
        for one_load in loads[h]:
            one_load.wait()
        coarse[:, cols] = halve(kv[:, cols])
        sends[2][:, cols] = halve(coarse[:, cols])
        if h == 0:
            pl.semaphore_wait(barrier, len(masks) + jnp.where(middle, 1, 0) + jnp.where(has_cross, 1, 0))
        second_out[h].start()
    to_sibling.start()
    to_inner.start()
    sends[3][:32, :] = halve(sends[2][...])
    third_early.start()
    sends[4][:16, :] = halve(sends[3][:32, :])
    when_start(middle, fourth_out[0])
    w_copy = pltpu.make_async_copy(w_hbm, w_vmem, w_sem)
    w_copy.start()
    q_load.wait()

    low_lanes = lax.broadcasted_iota(jnp.int32, (TILE, LANES), 1) < DH
    one = jnp.ones((TILE, LANES), jnp.bfloat16)
    zero = jnp.zeros((TILE, LANES), jnp.bfloat16)
    low_ones = jnp.where(low_lanes, one, zero)
    high_ones = jnp.where(low_lanes, zero, one)

    def columns(h, pair):
        at = parts[h].start + (pair - h * (pairs // 2)) * LANES
        return (pl.ds(pl.multiple_of(at, LANES), LANES),
                pl.ds(pl.multiple_of(at + part, LANES), LANES))

    def score(left_side, spots, key_cols):
        right_side = jnp.concatenate(
            [jnp.concatenate([ref[base : base + TILE, key_cols], ref[base : base + TILE, seg_columns]],
                             axis=1) for ref, base in spots], axis=0)
        return lax.dot_general(left_side, right_side, (((1,), (1,)), ((), ())),
                               preferred_element_type=jnp.float32)

    def highest(scores):
        top = scores[:, :LANES]
        for at in range(LANES, scores.shape[1], LANES):
            top = jnp.maximum(top, scores[:, at : at + LANES])
        return jnp.broadcast_to(jnp.max(top, axis=1, keepdims=True), top.shape)

    def weigh(scores, top, spots, value_cols):
        half = top.shape[0] // 2
        left_side, right_side = [], []
        for index, (ref, base) in enumerate(spots):
            some = scores[:, index * LANES : (index + 1) * LANES]
            weights = jnp.exp(some - top).astype(jnp.bfloat16)
            values = ref[base : base + TILE, value_cols]
            left_side += [weights[:half], weights[half:]]
            right_side += [
                jnp.concatenate([jnp.where(low_lanes, values, zero), low_ones], axis=1),
                jnp.concatenate([jnp.where(low_lanes, zero, values), high_ones], axis=1),
            ]
        return jnp.dot(jnp.concatenate(left_side, axis=1), jnp.concatenate(right_side, axis=0),
                       preferred_element_type=jnp.float32)

    def rescale(old, top):
        shrink = jnp.exp(old - top)
        half = top.shape[0] // 2
        lanes = lax.broadcasted_iota(jnp.int32, (half, LANES), 1) < DH
        both = jnp.where(lanes, shrink[:half], shrink[half:])
        return jnp.concatenate([both, both], axis=1)

    def whole_step(h, pair, spots):
        key_cols, value_cols = columns(h, pair)
        left_side = jnp.concatenate([queries[pair], query_seg[...]], axis=1)
        scores = score(left_side, spots, key_cols)
        old = largest[pair]
        top = jnp.maximum(old, highest(scores))
        largest[pair] = top
        total[pair] = total[pair] * rescale(old, top) + weigh(scores, top, spots, value_cols)

    def tile_step(h, pair, start, spots, last):
        key_cols, value_cols = columns(h, pair)
        heads = (pl.ds(start, TILE), pl.ds(pl.multiple_of(start + tokens, TILE), TILE))
        left_side = jnp.concatenate(
            [jnp.concatenate([queries[pair, head], query_seg[head, :]], axis=1) for head in heads], axis=0)
        scores = score(left_side, spots, key_cols)
        old = jnp.concatenate([largest[pair, head] for head in heads], axis=0)
        top = jnp.maximum(old, highest(scores))
        acc = total[pair, heads[0]] * rescale(old, top) + weigh(scores, top, spots, value_cols)
        if last:
            context[heads[0], pl.ds(pl.multiple_of(pair * LANES, LANES), LANES)] = (
                acc[:, :LANES] / acc[:, LANES:]).astype(jnp.bfloat16)
        else:
            for index, head in enumerate(heads):
                largest[pair, head] = top[index * TILE : (index + 1) * TILE]
            total[pair, heads[0]] = acc

    def halves(body):
        for h in range(2):
            pl.loop(h * (pairs // 2), (h + 1) * (pairs // 2), unroll=4)(functools.partial(body, h))

    near = [(kv, 0), (kv, TILE), (blocks[1], 0)]

    def first_step(h, pair):
        key_cols, value_cols = columns(h, pair)
        scaled = q_ref[:, pl.ds(pl.multiple_of(pair * LANES, LANES), LANES)] * jnp.bfloat16(DH**-0.5)
        lanes = lax.broadcasted_iota(jnp.int32, (tokens, LANES), 1) < DH
        none = jnp.zeros_like(scaled)
        both = jnp.concatenate([jnp.where(lanes, scaled, none), jnp.where(lanes, none, scaled)], axis=0)
        queries[pair] = both
        scores = score(jnp.concatenate([both, query_seg[...]], axis=1), near, key_cols)
        top = highest(scores)
        largest[pair] = top
        total[pair] = weigh(scores, top, near, value_cols)

    def relay(index):
        @pl.when(middle)
        def _():
            fourth_out[index].wait_recv()
            fourth_away[index].start()
            fourth_on[index].start()

    to_sibling.wait_recv()
    for h, cols in enumerate(parts):
        pl.loop(h * (pairs // 2), (h + 1) * (pairs // 2), unroll=4)(functools.partial(first_step, h))
        if h == 0:
            third_early.wait_recv()
            third_early_on.start()
            sends[4][32:48, :] = halve(blocks[3][pl.ds(mine, 32), :])
            when_start(middle, fourth_out[1])
        second_out[h].wait_recv()
        second_on[h].start()
        sends[3][32:, cols] = halve(blocks[2][pl.ds(mine, HALF), cols])
        third_out[h].start()
        sends[4][16:32, cols] = halve(sends[3][32:, cols])
        when_start(middle, fourth_out[2 + h])
        when_start(has_cross, to_cross[h])
        relay(h)

    to_inner.wait_recv()
    halves(lambda h, pair: tile_step(h, pair, inner_row, [(inner, 0)], False))

    for h, cols in enumerate(parts):
        third_out[h].wait_recv()
        third_on[h].start()
        sends[4][48:, cols] = halve(blocks[3][pl.ds(pl.multiple_of(mine + 32, 32), 32), cols])
        when_start(middle, fourth_out[4 + h])

    @pl.when(side)
    def _():
        for index in range(2):
            fourth_away[index].wait_recv()
            fourth_over[index].start()
            fourth_on[index].start()

    for copy in second_on + [third_early_on] + third_on:
        copy.wait_recv()
    halves(lambda h, pair: whole_step(h, pair, [(blocks[2], 0), (blocks[3], 0)]))

    @pl.when(to_side)
    def _():
        for index in range(2, 6):
            fourth_out[index].wait_recv()
            fourth_away[index].start()
            fourth_on[index].start()

    @pl.when(jnp.logical_and(middle, jnp.logical_not(straight)))
    def _():
        for index in range(2, 6):
            fourth_out[index].wait_recv()
            fourth_on[index].start()

    @pl.when(corner)
    def _():
        for index in range(2):
            fourth_away[index].wait_recv()
            fourth_on[index].start()
        for index in range(2):
            fourth_over[index].wait_recv()
            fourth_on[2 + 2 * index].start()
            fourth_on[3 + 2 * index].start()

    @pl.when(side)
    def _():
        for index in range(2, 6):
            fourth_away[index].wait_recv()
            fourth_on[index].start()

    for level in range(5, levels + 1):
        sends[level][:32, :] = halve(sends[level - 1][...])
        sends[level][32:, :] = halve(blocks[level - 1][pl.ds(mine, HALF), :])
        later_out[level].start()
        later_out[level].wait_recv()
        later_on[level].start()

    for copy in fourth_on + list(later_on.values()):
        copy.wait_recv()
    far = [(blocks[level], 0) for level in range(4, levels + 1)]
    halves(lambda h, pair: tile_step(h, pair, inner_row, far, True))

    @pl.when(has_cross)
    def _():
        for copy in to_cross:
            copy.wait_recv()

    halves(lambda h, pair: tile_step(h, pair, cross_row, far + [(cross, 0)], True))

    w_copy.wait()

    @pl.loop(0, out_ref.shape[1] // 256, unroll=4)
    def _(block):
        cols = pl.ds(pl.multiple_of(block * 256, 256), 256)
        out_ref[:, cols] = jnp.dot(context[...], w_vmem[:, cols],
                                   preferred_element_type=jnp.float32).astype(jnp.bfloat16)

    for copy in [to_sibling, to_inner, third_early, third_early_on] + second_out + second_on + third_out + third_on:
        copy.wait_send()
    for copy in fourth_on + list(later_out.values()) + list(later_on.values()):
        copy.wait_send()

    @pl.when(middle)
    def _():
        for copy in fourth_out + fourth_away[:2]:
            copy.wait_send()

    @pl.when(to_side)
    def _():
        for copy in fourth_away[2:]:
            copy.wait_send()

    @pl.when(side)
    def _():
        for copy in fourth_over:
            copy.wait_send()

    @pl.when(has_cross)
    def _():
        for copy in to_cross:
            copy.wait_send()


def on_device(devices, query_rows, key_rows, value_rows, segment_ids, out_weight):
    tokens, width = query_rows.shape
    levels = devices.bit_length() - 1
    span = 2 * width + LANES
    copies = 34 + 2 * (levels - 4)
    pairs = width // LANES
    bf16 = jnp.bfloat16
    scratch = [
        pltpu.VMEM((tokens, width), bf16),
        pltpu.VMEM((1, tokens), jnp.int32),
        pltpu.SemaphoreType.DMA((6,)),
        pltpu.VMEM((tokens, span), bf16),
        pltpu.VMEM((TILE, span), bf16),
        pltpu.VMEM((TILE, span), bf16),
        pltpu.VMEM((TILE, span), bf16),
        pltpu.VMEM((pairs, 2 * tokens, LANES), bf16),
        pltpu.VMEM((2 * tokens, LANES), bf16),
        pltpu.VMEM((pairs, 2 * tokens, LANES), jnp.float32),
        pltpu.VMEM((pairs, tokens, 2 * LANES), jnp.float32),
        pltpu.VMEM((tokens, width), bf16),
        pltpu.VMEM(out_weight.shape, bf16),
        pltpu.SemaphoreType.DMA,
        pltpu.SemaphoreType.DMA((copies,)),
        pltpu.SemaphoreType.DMA((copies,)),
    ]
    scratch += [pltpu.VMEM((HALF, span), bf16) for _ in range(2, levels + 1)]
    scratch += [pltpu.VMEM((TILE, span), bf16) for _ in range(1, levels + 1)]
    vmem = pl.BlockSpec(memory_space=pltpu.VMEM)
    return pl.pallas_call(
        functools.partial(attend, devices),
        out_shape=jax.ShapeDtypeStruct((tokens, width), bf16),
        in_specs=[pl.BlockSpec(memory_space=pltpu.HBM)] * 5,
        out_specs=vmem,
        scratch_shapes=scratch,
        compiler_params=pltpu.CompilerParams(
            collective_id=0, has_side_effects=True),
    )(query_rows, key_rows, value_rows, segment_ids.reshape(1, tokens), out_weight)


def solution(mesh):
    rows = P(("groups", "seq"), None)
    return jax.shard_map(
        functools.partial(on_device, mesh.shape["seq"]), mesh=mesh,
        in_specs=(rows, rows, rows, P(("groups", "seq")), P()),
        out_specs=rows, check_vma=False)
```

```python
import functools
import jax
import jax.numpy as jnp
from jax import lax
from jax.experimental import pallas as pl
from jax.experimental.pallas import tpu as pltpu
from jax.sharding import PartitionSpec as P

DH = 64
TILE = 128
LANES = 128
HALF = 64
BIG = 2.0**100
MESH = pl.DeviceIdType.MESH


def flip(index, mask):
    bit = 0
    while (1 << bit) <= mask:
        if mask & (1 << bit):
            index = index + (1 - 2 * ((index // (1 << bit)) % 2)) * (1 << bit)
        bit += 1
    return index


def halve(source):
    rows = source.shape[0]
    row = lax.broadcasted_iota(jnp.int32, (rows // 2, rows), 0)
    col = lax.broadcasted_iota(jnp.int32, (rows // 2, rows), 1)
    pick = jnp.where(col // 2 == row, 0.5, 0.0).astype(jnp.bfloat16)
    return jnp.dot(pick, source, preferred_element_type=jnp.float32).astype(jnp.bfloat16)


def attend(devices, q_hbm, k_hbm, v_hbm, seg_hbm, w_hbm, out_ref, q_ref, seg_ref, load_sem, kv, coarse, inner, cross,
           queries, query_seg, largest, total, context, w_vmem, w_sem, send_sem, recv_sem, own_seg, inner_seg, cross_seg, far_seg,
           count_out, count_in, partial, *rest):
    levels = devices.bit_length() - 1
    sends = dict(zip(range(2, levels + 1), rest))
    blocks = dict(zip(range(1, levels + 1), rest[levels - 1 :]))
    me = lax.axis_index("seq")
    core = me % 2
    tokens, width = q_hbm.shape
    pairs = width // LANES
    part = width // 2
    parts = (slice(0, 2 * part), slice(2 * part, 4 * part))
    every = slice(0, 4 * part)

    middle = (me // 4 + me // 8) % 2 == 1
    outer = jnp.logical_not(middle)
    straight = (me // 2 + me // 4) % 2 == 0
    corner = jnp.logical_and(outer, straight)
    side = jnp.logical_and(outer, jnp.logical_not(straight))
    to_side = jnp.logical_and(middle, straight)
    has_cross = jnp.logical_and(me + core > 0, me + core < devices)
    neighbour = me - 1 + 2 * core
    inner_row = pl.multiple_of((1 - core) * TILE, TILE)
    cross_row = pl.multiple_of(core * TILE, TILE)
    mine = pl.multiple_of(core * HALF, HALF)

    barrier = pltpu.get_barrier_semaphore()
    masks = [1, 2, 4] + [1 << (level - 1) for level in range(5, levels + 1)]
    for mask in masks:
        pl.semaphore_signal(barrier, inc=1, device_id={"seq": flip(me, mask)}, device_id_type=MESH)

    @pl.when(middle)
    def _():
        pl.semaphore_signal(barrier, inc=1, device_id={"seq": flip(me, 12)}, device_id_type=MESH)

    @pl.when(has_cross)
    def _():
        pl.semaphore_signal(barrier, inc=1, device_id={"seq": neighbour}, device_id_type=MESH)

    def load(source, index, from_cols, to_cols):
        return pltpu.make_async_copy(source.at[:, from_cols], kv.at[:, to_cols], load_sem.at[index])

    seg_load = pltpu.make_async_copy(seg_hbm, seg_ref, load_sem.at[0])
    q_load = pltpu.make_async_copy(q_hbm, q_ref, load_sem.at[1])
    loads = []
    for h in range(2):
        base = parts[h].start
        loads.append([
            load(k_hbm, 2 + 2 * h, slice(h * part, (h + 1) * part), slice(base, base + part)),
            load(v_hbm, 3 + 2 * h, slice(h * part, (h + 1) * part),
                 slice(base + part, base + 2 * part)),
        ])
    for some in loads[:1]:
        for one_load in some:
            one_load.start()
    seg_load.start()
    for some in loads[1:]:
        for one_load in some:
            one_load.start()
    q_load.start()

    made = []

    def remote(source, target, device):
        index = len(made)
        copy = pltpu.make_async_remote_copy(
            src_ref=source, dst_ref=target, send_sem=send_sem.at[index],
            recv_sem=recv_sem.at[index], device_id={"seq": device}, device_id_type=MESH)
        made.append(copy)
        return copy

    def send_count(slot, to_slot, device):
        return remote(count_out.at[slot], count_in.at[to_slot], device)

    def store_count(slot, low, high):
        spot = lax.broadcasted_iota(jnp.int32, (8, LANES), 0)
        count_out[slot] = jnp.where(spot == 0, low, high)

    def counts(slot):
        return count_in[slot, 0:1, :], count_in[slot, 1:2, :]

    def wider(level):
        low, high = counts(level)
        store_count(level + 1, count_out[level, 0:1, :] + low, count_out[level, 1:2, :] + high)

    def seg_rows(start, length, low, high):
        def at(token):
            return jnp.where(token >= low, 1, 0) + jnp.where(token >= high, 1, 0)

        at_first = at(start)
        kind = at_first if length == 1 else jnp.where(at_first == at(start + (length - 1.0)), at_first, 3)
        lane = lax.broadcasted_iota(jnp.int32, start.shape, 1)
        return jnp.where(lane == kind, -BIG, 0.0).astype(jnp.bfloat16)

    def tile_rows(at):
        row = lax.broadcasted_iota(jnp.int32, (TILE, LANES), 0)
        return (row + at).astype(jnp.float32)

    def far_rows(level):
        row = lax.broadcasted_iota(jnp.int32, (TILE, LANES), 0)
        if level == 1:
            start = row * 2
        else:
            size = TILE >> (level - 1)
            low_bits = HALF - 1
            piece = jnp.bitwise_and(row, low_bits) >> (size.bit_length() - 1)
            place = jnp.bitwise_xor(me % (1 << (level - 1)) - core, piece * 2)
            if level == 4:
                place = jnp.bitwise_xor(place, jnp.where(middle, 4, 0))
            if level > 4:
                place = jnp.bitwise_xor(place, jnp.bitwise_and(piece, 4) * jnp.where(middle, 1, 0))
            if level == 2:
                place = piece * 0
            place = place + (row >> 6)
            start = place * tokens + jnp.bitwise_and(row, size - 1) * (1 << level)
        low, high = counts(level)
        far_seg[level - 1] = seg_rows(start.astype(jnp.float32), 1 << level, low, high)

    def block_part(level, start, rows, cols):
        return blocks[level].at[pl.ds(pl.multiple_of(mine + start, 16), rows), cols]

    def exchange(level, start, rows, cols, mask):
        return remote(sends[level].at[start : start + rows, cols],
                      block_part(level, start, rows, cols), flip(me, mask))

    def forward(level, start, rows, cols, mask=1):
        here = block_part(level, start, rows, cols)
        return remote(here, here, flip(me, mask))

    to_sibling = remote(coarse, blocks[1], flip(me, 1))
    to_inner = remote(kv.at[pl.ds(inner_row, TILE)], inner, flip(me, 1))
    cross_first = [
        remote(source.at[pl.ds(cross_row, TILE), 0:part], cross.at[:, at : at + part], neighbour)
        for source, at in ((k_hbm, 0), (v_hbm, part))]
    cross_second = remote(kv.at[pl.ds(cross_row, TILE), parts[1]], cross.at[:, parts[1]], neighbour)
    count_cross = send_count(1, 0, neighbour)
    count_copies = [send_count(level, level, flip(me, 1 << (level - 1))) for level in range(1, 4)]
    count_middle = send_count(4, 4, flip(me, 12))
    count_away = remote(count_in.at[4], count_in.at[4], flip(me, 4))
    count_later = [send_count(level, level, flip(me, 1 << (level - 1))) for level in range(5, levels + 1)]
    second_out = [exchange(2, 0, HALF, cols, 2) for cols in parts]
    second_on = [forward(2, 0, HALF, cols) for cols in parts]
    third_early = exchange(3, 0, 32, every, 4)
    third_early_on = forward(3, 0, 32, every)
    third_out = [exchange(3, 32, 32, cols, 4) for cols in parts]
    third_on = [forward(3, 32, 32, cols) for cols in parts]
    pieces = [(0, every), (32, every), (16, parts[0]), (16, parts[1]), (48, parts[0]), (48, parts[1])]
    fourth_out = [exchange(4, start, 16, cols, 12) for start, cols in pieces]
    fourth_on = [forward(4, start, 16, cols) for start, cols in pieces]
    fourth_away = [forward(4, start, 16, cols, 4) for start, cols in pieces]
    fourth_over = [remote(block_part(4, start, 16, every), block_part(4, start + 16, 16, every), flip(me, 2))
                   for start in (0, 32)]
    later_out = {level: exchange(level, 0, HALF, every, 1 << (level - 1))
                 for level in range(5, levels + 1)}
    later_on = {level: forward(level, 0, HALF, every) for level in range(5, levels + 1)}

    def when_start(condition, copy):
        pl.when(condition)(copy.start)

    seg_load.wait()
    seg = seg_ref[...]
    first = jnp.sum(jnp.where(seg < 1, 1.0, 0.0), axis=1, keepdims=True)
    second = jnp.sum(jnp.where(seg < 2, 1.0, 0.0), axis=1, keepdims=True)
    store_count(1, first, second)
    pl.semaphore_wait(barrier, len(masks) + jnp.where(middle, 1, 0) + jnp.where(has_cross, 1, 0))

    @pl.when(has_cross)
    def _():
        for copy in cross_first:
            copy.start()
        count_cross.start()

    count_copies[0].start()
    for h, cols in enumerate(parts):
        for one_load in loads[h]:
            one_load.wait()
        coarse[:, cols] = halve(kv[:, cols])
        sends[2][:, cols] = halve(coarse[:, cols])
        second_out[h].start()
    to_sibling.start()
    to_inner.start()
    sends[3][:32, :] = halve(sends[2][...])
    third_early.start()
    sends[4][:16, :] = halve(sends[3][:32, :])
    when_start(middle, fourth_out[0])

    for at in (0, TILE):
        own_seg[at : at + TILE, :] = seg_rows(tile_rows(at), 1, first, second)
    lane = lax.broadcasted_iota(jnp.int32, (tokens, LANES), 1)
    other = jnp.where(lane < 4, jnp.where(own_seg[...].astype(jnp.float32) < 0, 0.0, 1.0), 0.0).astype(jnp.bfloat16)
    query_seg[:tokens, :] = other
    query_seg[tokens:, :] = other

    @pl.when(jnp.logical_not(has_cross))
    def _():
        cross[...] = jnp.zeros(cross.shape, cross.dtype)
        spot = lax.broadcasted_iota(jnp.int32, (TILE, LANES), 1)
        cross_seg[...] = jnp.where(spot == 3, -BIG, 0.0).astype(jnp.bfloat16)

    w_copy = pltpu.make_async_copy(w_hbm, w_vmem, w_sem)
    w_copy.start()
    count_copies[0].wait_recv()
    wider(1)
    count_copies[1].start()
    far_rows(1)
    low, high = counts(1)
    inner_seg[...] = seg_rows(tile_rows(cross_row), 1, low, high)
    q_load.wait()

    low_lanes = lax.broadcasted_iota(jnp.int32, (TILE, LANES), 1) < DH
    one = jnp.ones((TILE, LANES), jnp.bfloat16)
    zero = jnp.zeros((TILE, LANES), jnp.bfloat16)
    low_ones = jnp.where(low_lanes, one, zero)
    high_ones = jnp.where(low_lanes, zero, one)

    def columns(h, pair):
        at = parts[h].start + (pair - h * (pairs // 2)) * LANES
        return (pl.ds(pl.multiple_of(at, LANES), LANES),
                pl.ds(pl.multiple_of(at + part, LANES), LANES))

    def score(left_side, spots, key_cols):
        right_side = jnp.concatenate(
            [jnp.concatenate([ref[base : base + TILE, key_cols], seg[base : base + TILE, :]], axis=1)
             for ref, seg, base in spots], axis=0)
        return lax.dot_general(left_side, right_side, (((1,), (1,)), ((), ())),
                               preferred_element_type=jnp.float32)

    def highest(scores):
        top = scores[:, :LANES]
        for at in range(LANES, scores.shape[1], LANES):
            top = jnp.maximum(top, scores[:, at : at + LANES])
        return jnp.broadcast_to(jnp.max(top, axis=1, keepdims=True), top.shape)

    def weigh(scores, top, spots, value_cols):
        half = top.shape[0] // 2
        left_side, right_side = [], []
        for index, (ref, _, base) in enumerate(spots):
            some = scores[:, index * LANES : (index + 1) * LANES]
            weights = jnp.exp(some - top).astype(jnp.bfloat16)
            values = ref[base : base + TILE, value_cols]
            left_side += [weights[:half], weights[half:]]
            right_side += [
                jnp.concatenate([jnp.where(low_lanes, values, zero), low_ones], axis=1),
                jnp.concatenate([jnp.where(low_lanes, zero, values), high_ones], axis=1),
            ]
        return jnp.dot(jnp.concatenate(left_side, axis=1), jnp.concatenate(right_side, axis=0),
                       preferred_element_type=jnp.float32)

    def rescale(old, top):
        shrink = jnp.exp(old - top)
        half = top.shape[0] // 2
        lanes = lax.broadcasted_iota(jnp.int32, (half, LANES), 1) < DH
        both = jnp.where(lanes, shrink[:half], shrink[half:])
        return jnp.concatenate([both, both], axis=1)

    def whole_step(h, pair, spots):
        key_cols, value_cols = columns(h, pair)
        left_side = jnp.concatenate([queries[pair], query_seg[...]], axis=1)
        scores = score(left_side, spots, key_cols)
        old = largest[pair]
        top = jnp.maximum(old, highest(scores))
        largest[pair] = top
        total[pair] = total[pair] * rescale(old, top) + weigh(scores, top, spots, value_cols)

    def tile_step(h, pair, start, spots, last):
        key_cols, value_cols = columns(h, pair)
        heads = (pl.ds(start, TILE), pl.ds(pl.multiple_of(start + tokens, TILE), TILE))
        left_side = jnp.concatenate(
            [jnp.concatenate([queries[pair, head], query_seg[head, :]], axis=1) for head in heads], axis=0)
        scores = score(left_side, spots, key_cols)
        old = jnp.concatenate([largest[pair, head] for head in heads], axis=0)
        top = jnp.maximum(old, highest(scores))
        acc = total[pair, heads[0]] * rescale(old, top) + weigh(scores, top, spots, value_cols)
        if last:
            context[heads[0], pl.ds(pl.multiple_of(pair * LANES, LANES), LANES)] = (
                acc[:, :LANES] / acc[:, LANES:]).astype(jnp.bfloat16)
        else:
            for index, head in enumerate(heads):
                largest[pair, head] = top[index * TILE : (index + 1) * TILE]
            total[pair, heads[0]] = acc

    def halves(body):
        for h in range(2):
            pl.loop(h * (pairs // 2), (h + 1) * (pairs // 2), unroll=4)(functools.partial(body, h))

    near = [(kv, own_seg, 0), (kv, own_seg, TILE), (blocks[1], far_seg.at[0], 0)]

    def first_step(h, pair):
        key_cols, value_cols = columns(h, pair)
        scaled = q_ref[:, pl.ds(pl.multiple_of(pair * LANES, LANES), LANES)] * jnp.bfloat16(DH**-0.5)
        lanes = lax.broadcasted_iota(jnp.int32, (tokens, LANES), 1) < DH
        none = jnp.zeros_like(scaled)
        both = jnp.concatenate([jnp.where(lanes, scaled, none), jnp.where(lanes, none, scaled)], axis=0)
        queries[pair] = both
        scores = score(jnp.concatenate([both, query_seg[...]], axis=1), near, key_cols)
        top = highest(scores)
        largest[pair] = top
        total[pair] = weigh(scores, top, near, value_cols)

    def relay(index, away=middle):
        @pl.when(middle)
        def _():
            fourth_out[index].wait_recv()
            fourth_on[index].start()

        @pl.when(away)
        def _():
            fourth_away[index].start()

    def span_of(h, body):
        pl.loop(h * (pairs // 2), (h + 1) * (pairs // 2), unroll=4)(functools.partial(body, h))

    def far_spots(some):
        return [(blocks[level], far_seg.at[level - 1], 0) for level in some]

    to_sibling.wait_recv()
    for h, cols in enumerate(parts):
        span_of(h, first_step)
        if h == 0:
            third_early.wait_recv()
            third_early_on.start()
            sends[4][32:48, :] = halve(blocks[3][pl.ds(mine, 32), :])
            when_start(middle, fourth_out[1])
        second_out[h].wait_recv()
        second_on[h].start()
        sends[3][32:, cols] = halve(blocks[2][pl.ds(mine, HALF), cols])
        third_out[h].start()
        sends[4][16:32, cols] = halve(sends[3][32:, cols])
        when_start(middle, fourth_out[2 + h])
        if h == 0:
            count_copies[1].wait_recv()
            wider(2)
            count_copies[2].start()
        else:
            when_start(has_cross, cross_second)
        relay(h)

    far_rows(2)
    to_inner.wait_recv()
    halves(lambda h, pair: tile_step(h, pair, inner_row, [(inner, inner_seg, 0)], False))

    count_copies[2].wait_recv()
    wider(3)
    when_start(middle, count_middle)
    far_rows(3)
    for h, cols in enumerate(parts):
        third_out[h].wait_recv()
        third_on[h].start()
        sends[4][48:, cols] = halve(blocks[3][pl.ds(pl.multiple_of(mine + 32, 32), 32), cols])
        when_start(middle, fourth_out[4 + h])
        relay(2 + h, to_side)

    @pl.when(outer)
    def _():
        for index in range(2):
            fourth_away[index].wait_recv()
            fourth_on[index].start()

    @pl.when(side)
    def _():
        for index in range(2):
            fourth_over[index].start()

    @pl.when(middle)
    def _():
        count_middle.wait_recv()
        count_away.start()

    for copy in second_on + [third_early_on] + third_on:
        copy.wait_recv()
    for h in range(2):
        span_of(h, lambda h, pair: whole_step(h, pair, far_spots((2, 3))))
        relay(4 + h, to_side)

    @pl.when(corner)
    def _():
        for index in range(2):
            fourth_over[index].wait_recv()
            fourth_on[2 + 2 * index].start()
            fourth_on[3 + 2 * index].start()

    pl.when(outer)(count_away.wait_recv)
    far_rows(4)

    @pl.when(has_cross)
    def _():
        count_cross.wait_recv()
        low, high = counts(0)
        cross_seg[...] = seg_rows(tile_rows(inner_row), 1, low, high)

    if levels > 4:
        @pl.when(side)
        def _():
            for index in range(2, 6):
                fourth_away[index].wait_recv()
                fourth_on[index].start()

        for level in range(5, levels + 1):
            wider(level - 1)
            count_later[level - 5].start()
            sends[level][:32, :] = halve(sends[level - 1][...])
            sends[level][32:, :] = halve(blocks[level - 1][pl.ds(mine, HALF), :])
            later_out[level].start()
            later_out[level].wait_recv()
            later_on[level].start()
            count_later[level - 5].wait_recv()
            far_rows(level)
        for copy in later_on.values():
            copy.wait_recv()
    far = far_spots(range(4, levels + 1))

    for h in range(2):
        if levels == 4:
            @pl.when(side)
            def _():
                for index in (2 + h, 4 + h):
                    fourth_away[index].wait_recv()
                    fourth_on[index].start()

        for index in ((0, 1) if h == 0 else ()) + (2 + h, 4 + h):
            fourth_on[index].wait_recv()
        span_of(h, lambda h, pair: tile_step(h, pair, inner_row, far, True))

        @pl.when(has_cross)
        def _():
            for copy in cross_first if h == 0 else [cross_second]:
                copy.wait_recv()

        span_of(h, lambda h, pair: tile_step(h, pair, cross_row, far + [(cross, cross_seg, 0)], True))
        if h == 0:
            w_copy.wait()

            @pl.loop(0, width // 256, unroll=4)
            def _(block):
                cols = pl.ds(pl.multiple_of(block * 256, 256), 256)
                partial[:, cols] = jnp.dot(context[:, :part], w_vmem[:part, cols],
                                           preferred_element_type=jnp.float32)

    @pl.loop(0, out_ref.shape[1] // 256, unroll=4)
    def _(block):
        cols = pl.ds(pl.multiple_of(block * 256, 256), 256)
        out_ref[:, cols] = (partial[:, cols] + jnp.dot(
            context[:, part:], w_vmem[part:, cols], preferred_element_type=jnp.float32)).astype(jnp.bfloat16)

    for copy in [to_sibling, to_inner, third_early, third_early_on] + second_out + second_on + third_out + third_on:
        copy.wait_send()
    for copy in count_copies + count_later + fourth_on + list(later_out.values()) + list(later_on.values()):
        copy.wait_send()

    @pl.when(middle)
    def _():
        for copy in fourth_out + fourth_away[:2] + [count_middle, count_away]:
            copy.wait_send()

    @pl.when(to_side)
    def _():
        for copy in fourth_away[2:]:
            copy.wait_send()

    @pl.when(side)
    def _():
        for copy in fourth_over:
            copy.wait_send()

    @pl.when(has_cross)
    def _():
        for copy in cross_first + [cross_second, count_cross]:
            copy.wait_send()


def on_device(devices, query_rows, key_rows, value_rows, segment_ids, out_weight):
    tokens, width = query_rows.shape
    levels = devices.bit_length() - 1
    span = 2 * width
    copies = 41 + 3 * (levels - 4)
    pairs = width // LANES
    bf16 = jnp.bfloat16
    scratch = [
        pltpu.VMEM((tokens, width), bf16),
        pltpu.VMEM((1, tokens), jnp.int32),
        pltpu.SemaphoreType.DMA((6,)),
        pltpu.VMEM((tokens, span), bf16),
        pltpu.VMEM((TILE, span), bf16),
        pltpu.VMEM((TILE, span), bf16),
        pltpu.VMEM((TILE, span), bf16),
        pltpu.VMEM((pairs, 2 * tokens, LANES), bf16),
        pltpu.VMEM((2 * tokens, LANES), bf16),
        pltpu.VMEM((pairs, 2 * tokens, LANES), jnp.float32),
        pltpu.VMEM((pairs, tokens, 2 * LANES), jnp.float32),
        pltpu.VMEM((tokens, width), bf16),
        pltpu.VMEM(out_weight.shape, bf16),
        pltpu.SemaphoreType.DMA,
        pltpu.SemaphoreType.DMA((copies,)),
        pltpu.SemaphoreType.DMA((copies,)),
        pltpu.VMEM((tokens, LANES), bf16),
        pltpu.VMEM((TILE, LANES), bf16),
        pltpu.VMEM((TILE, LANES), bf16),
        pltpu.VMEM((levels, TILE, LANES), bf16),
        pltpu.VMEM((levels + 2, 8, LANES), jnp.float32),
        pltpu.VMEM((levels + 1, 8, LANES), jnp.float32),
        pltpu.VMEM((tokens, width), jnp.float32),
    ]
    scratch += [pltpu.VMEM((HALF, span), bf16) for _ in range(2, levels + 1)]
    scratch += [pltpu.VMEM((TILE, span), bf16) for _ in range(1, levels + 1)]
    vmem = pl.BlockSpec(memory_space=pltpu.VMEM)
    return pl.pallas_call(
        functools.partial(attend, devices),
        out_shape=jax.ShapeDtypeStruct((tokens, width), bf16),
        in_specs=[pl.BlockSpec(memory_space=pltpu.HBM)] * 5,
        out_specs=vmem,
        scratch_shapes=scratch,
        compiler_params=pltpu.CompilerParams(
            collective_id=0, has_side_effects=True),
    )(query_rows, key_rows, value_rows, segment_ids.reshape(1, tokens), out_weight)


def solution(mesh):
    rows = P(("groups", "seq"), None)
    return jax.shard_map(
        functools.partial(on_device, mesh.shape["seq"]), mesh=mesh,
        in_specs=(rows, rows, rows, P(("groups", "seq")), P()),
        out_specs=rows, check_vma=False)
```

```python
import functools
import jax
import jax.numpy as jnp
from jax import lax
from jax.experimental import pallas as pl
from jax.experimental.pallas import tpu as pltpu
from jax.sharding import PartitionSpec as P

DH = 64
TILE = 128
LANES = 128
HALF = 64
BIG = 2.0**100
MESH = pl.DeviceIdType.MESH


def flip(index, mask):
    bit = 0
    while (1 << bit) <= mask:
        if mask & (1 << bit):
            index = index + (1 - 2 * ((index // (1 << bit)) % 2)) * (1 << bit)
        bit += 1
    return index


def halve(source):
    rows = source.shape[0]
    row = lax.broadcasted_iota(jnp.int32, (rows // 2, rows), 0)
    col = lax.broadcasted_iota(jnp.int32, (rows // 2, rows), 1)
    pick = jnp.where(col // 2 == row, 0.5, 0.0).astype(jnp.bfloat16)
    return jnp.dot(pick, source, preferred_element_type=jnp.float32).astype(jnp.bfloat16)


def attend(devices, q_hbm, k_hbm, v_hbm, seg_hbm, w_hbm, out_ref, q_ref, seg_ref, load_sem, kv, coarse, inner, cross,
           queries, query_seg, largest, total, context, w_vmem, w_sem, send_sem, recv_sem, *rest):
    levels = devices.bit_length() - 1
    sends = dict(zip(range(2, levels + 1), rest))
    blocks = dict(zip(range(1, levels + 1), rest[levels - 1 :]))
    me = lax.axis_index("seq")
    core = me % 2
    tokens, width = q_hbm.shape
    pairs = width // LANES
    part = width // 2
    seg_at = 2 * part
    parts = (slice(0, 2 * part), slice(2 * part, 4 * part + LANES))
    starts = (0, 2 * part + LANES)
    every = slice(0, 4 * part + LANES)
    seg_columns = slice(seg_at, seg_at + LANES)

    middle = (me // 4 + me // 8) % 2 == 1
    outer = jnp.logical_not(middle)
    straight = (me // 2 + me // 4) % 2 == 0
    corner = jnp.logical_and(outer, straight)
    side = jnp.logical_and(outer, jnp.logical_not(straight))
    to_side = jnp.logical_and(middle, straight)
    has_cross = jnp.logical_and(me + core > 0, me + core < devices)
    neighbour = me - 1 + 2 * core
    inner_row = pl.multiple_of((1 - core) * TILE, TILE)
    cross_row = pl.multiple_of(core * TILE, TILE)
    mine = pl.multiple_of(core * HALF, HALF)

    barrier = pltpu.get_barrier_semaphore()
    masks = [1, 2, 4] + [1 << (level - 1) for level in range(5, levels + 1)]
    for mask in masks:
        pl.semaphore_signal(barrier, inc=1, device_id={"seq": flip(me, mask)}, device_id_type=MESH)

    @pl.when(middle)
    def _():
        pl.semaphore_signal(barrier, inc=1, device_id={"seq": flip(me, 12)}, device_id_type=MESH)

    @pl.when(has_cross)
    def _():
        pl.semaphore_signal(barrier, inc=1, device_id={"seq": neighbour}, device_id_type=MESH)

    def load(source, index, from_cols, to_cols):
        return pltpu.make_async_copy(source.at[:, from_cols], kv.at[:, to_cols], load_sem.at[index])

    seg_load = pltpu.make_async_copy(seg_hbm, seg_ref, load_sem.at[0])
    q_load = pltpu.make_async_copy(q_hbm, q_ref, load_sem.at[1])
    loads = []
    for h in range(2):
        base = starts[h]
        loads.append([
            load(k_hbm, 2 + 2 * h, slice(h * part, (h + 1) * part), slice(base, base + part)),
            load(v_hbm, 3 + 2 * h, slice(h * part, (h + 1) * part),
                 slice(base + part, base + 2 * part)),
        ])
    for some in loads:
        for one_load in some:
            one_load.start()
        if some is loads[0]:
            seg_load.start()
    q_load.start()
    made = []

    def remote(source, target, device):
        index = len(made)
        copy = pltpu.make_async_remote_copy(
            src_ref=source, dst_ref=target, send_sem=send_sem.at[index],
            recv_sem=recv_sem.at[index], device_id={"seq": device}, device_id_type=MESH)
        made.append(copy)
        return copy

    def block_part(level, start, rows, cols):
        return blocks[level].at[pl.ds(pl.multiple_of(mine + start, 16), rows), cols]

    def exchange(level, start, rows, cols, mask):
        return remote(sends[level].at[start : start + rows, cols],
                      block_part(level, start, rows, cols), flip(me, mask))

    def forward(level, start, rows, cols, mask=1):
        here = block_part(level, start, rows, cols)
        return remote(here, here, flip(me, mask))

    to_sibling = remote(coarse, blocks[1], flip(me, 1))
    to_inner = remote(kv.at[pl.ds(inner_row, TILE)], inner, flip(me, 1))
    to_cross = [remote(kv.at[pl.ds(cross_row, TILE), cols], cross.at[:, cols], neighbour)
                for cols in parts]
    second_out = [exchange(2, 0, HALF, cols, 2) for cols in parts]
    second_on = [forward(2, 0, HALF, cols) for cols in parts]
    third_early = exchange(3, 0, 32, every, 4)
    third_early_on = forward(3, 0, 32, every)
    third_out = [exchange(3, 32, 32, cols, 4) for cols in parts]
    third_on = [forward(3, 32, 32, cols) for cols in parts]
    pieces = [(0, every), (32, every), (16, parts[0]), (16, parts[1]), (48, parts[0]), (48, parts[1])]
    fourth_out = [exchange(4, start, 16, cols, 12) for start, cols in pieces]
    fourth_on = [forward(4, start, 16, cols) for start, cols in pieces]
    fourth_away = [forward(4, start, 16, cols, 4) for start, cols in pieces]
    fourth_over = [remote(block_part(4, start, 16, every), block_part(4, start + 16, 16, every), flip(me, 2))
                   for start in (0, 32)]
    later_out = {level: exchange(level, 0, HALF, every, 1 << (level - 1))
                 for level in range(5, levels + 1)}
    later_on = {level: forward(level, 0, HALF, every) for level in range(5, levels + 1)}

    def when_start(condition, copy):
        pl.when(condition)(copy.start)

    def set_seg():
        seg_load.wait()

        seg = seg_ref[...]
        first = jnp.sum(jnp.where(seg < 1, 1.0, 0.0), axis=1, keepdims=True)
        second = jnp.sum(jnp.where(seg < 2, 1.0, 0.0), axis=1, keepdims=True)
        row = lax.broadcasted_iota(jnp.int32, (tokens, LANES), 0).astype(jnp.float32)
        lane = lax.broadcasted_iota(jnp.int32, (tokens, LANES), 1).astype(jnp.float32)
        row_seg = jnp.where(row >= first, 1.0, 0.0) + jnp.where(row >= second, 1.0, 0.0)
        kv[:, seg_columns] = jnp.where(lane == row_seg, -BIG, 0.0).astype(jnp.bfloat16)
        other = jnp.where(lane == row_seg, 0.0, jnp.where(lane < 4, 1.0, 0.0)).astype(jnp.bfloat16)
        query_seg[:tokens, :] = other
        query_seg[tokens:, :] = other

    for h, cols in enumerate(parts):
        if h == 1:
            set_seg()
        for one_load in loads[h]:
            one_load.wait()
        coarse[:, cols] = halve(kv[:, cols])
        sends[2][:, cols] = halve(coarse[:, cols])
        if h == 0:
            pl.semaphore_wait(barrier, len(masks) + jnp.where(middle, 1, 0) + jnp.where(has_cross, 1, 0))
        second_out[h].start()
    to_sibling.start()
    to_inner.start()
    sends[3][:32, :] = halve(sends[2][...])
    third_early.start()
    sends[4][:16, :] = halve(sends[3][:32, :])
    when_start(middle, fourth_out[0])

    @pl.when(jnp.logical_not(has_cross))
    def _():
        cross[...] = jnp.zeros(cross.shape, cross.dtype)
        spot = lax.broadcasted_iota(jnp.int32, (TILE, LANES), 1)
        cross[:, seg_columns] = jnp.where(spot == 3, -BIG, 0.0).astype(jnp.bfloat16)

    w_copy = pltpu.make_async_copy(w_hbm, w_vmem, w_sem)
    w_copy.start()
    q_load.wait()

    low_lanes = lax.broadcasted_iota(jnp.int32, (TILE, LANES), 1) < DH
    one = jnp.ones((TILE, LANES), jnp.bfloat16)
    zero = jnp.zeros((TILE, LANES), jnp.bfloat16)
    low_ones = jnp.where(low_lanes, one, zero)
    high_ones = jnp.where(low_lanes, zero, one)

    def columns(h, pair):
        at = starts[h] + (pair - h * (pairs // 2)) * LANES
        return (pl.ds(pl.multiple_of(at, LANES), LANES),
                pl.ds(pl.multiple_of(at + part, LANES), LANES))

    def score(left_side, spots, key_cols):
        right_side = jnp.concatenate(
            [jnp.concatenate([ref[base : base + TILE, key_cols], ref[base : base + TILE, seg_columns]],
                             axis=1) for ref, base in spots], axis=0)
        return lax.dot_general(left_side, right_side, (((1,), (1,)), ((), ())),
                               preferred_element_type=jnp.float32)

    def highest(scores):
        top = scores[:, :LANES]
        for at in range(LANES, scores.shape[1], LANES):
            top = jnp.maximum(top, scores[:, at : at + LANES])
        return jnp.broadcast_to(jnp.max(top, axis=1, keepdims=True), top.shape)

    def weigh(scores, top, spots, value_cols):
        half = top.shape[0] // 2
        left_side, right_side = [], []
        for index, (ref, base) in enumerate(spots):
            some = scores[:, index * LANES : (index + 1) * LANES]
            weights = jnp.exp(some - top).astype(jnp.bfloat16)
            values = ref[base : base + TILE, value_cols]
            left_side += [weights[:half], weights[half:]]
            right_side += [
                jnp.concatenate([jnp.where(low_lanes, values, zero), low_ones], axis=1),
                jnp.concatenate([jnp.where(low_lanes, zero, values), high_ones], axis=1),
            ]
        return jnp.dot(jnp.concatenate(left_side, axis=1), jnp.concatenate(right_side, axis=0),
                       preferred_element_type=jnp.float32)

    def rescale(old, top):
        shrink = jnp.exp(old - top)
        half = top.shape[0] // 2
        lanes = lax.broadcasted_iota(jnp.int32, (half, LANES), 1) < DH
        both = jnp.where(lanes, shrink[:half], shrink[half:])
        return jnp.concatenate([both, both], axis=1)

    def whole_step(h, pair, spots):
        key_cols, value_cols = columns(h, pair)
        left_side = jnp.concatenate([queries[pair], query_seg[...]], axis=1)
        scores = score(left_side, spots, key_cols)
        yield
        old = largest[pair]
        top = jnp.maximum(old, highest(scores))
        yield
        largest[pair] = top
        total[pair] = total[pair] * rescale(old, top) + weigh(scores, top, spots, value_cols)

    def tile_step(h, pair, start, spots, last):
        key_cols, value_cols = columns(h, pair)
        heads = (pl.ds(start, TILE), pl.ds(pl.multiple_of(start + tokens, TILE), TILE))
        left_side = jnp.concatenate(
            [jnp.concatenate([queries[pair, head], query_seg[head, :]], axis=1) for head in heads], axis=0)
        scores = score(left_side, spots, key_cols)
        yield
        old = jnp.concatenate([largest[pair, head] for head in heads], axis=0)
        top = jnp.maximum(old, highest(scores))
        yield
        acc = total[pair, heads[0]] * rescale(old, top) + weigh(scores, top, spots, value_cols)
        if last:
            context[heads[0], pl.ds(pl.multiple_of(pair * LANES, LANES), LANES)] = (
                acc[:, :LANES] / acc[:, LANES:]).astype(jnp.bfloat16)
        else:
            for index, head in enumerate(heads):
                largest[pair, head] = top[index * TILE : (index + 1) * TILE]
            total[pair, heads[0]] = acc

    def run(steps):
        for _ in range(3):
            for step in steps:
                next(step, None)

    def halves(body):
        run([body(pair // (pairs // 2), pair) for pair in range(pairs)])

    near = [(kv, 0), (kv, TILE), (blocks[1], 0)]

    def first_step(h, pair):
        key_cols, value_cols = columns(h, pair)
        scaled = q_ref[:, pl.ds(pl.multiple_of(pair * LANES, LANES), LANES)] * jnp.bfloat16(DH**-0.5)
        lanes = lax.broadcasted_iota(jnp.int32, (tokens, LANES), 1) < DH
        none = jnp.zeros_like(scaled)
        both = jnp.concatenate([jnp.where(lanes, scaled, none), jnp.where(lanes, none, scaled)], axis=0)
        queries[pair] = both
        scores = score(jnp.concatenate([both, query_seg[...]], axis=1), near, key_cols)
        yield
        top = highest(scores)
        yield
        largest[pair] = top
        total[pair] = weigh(scores, top, near, value_cols)

    def relay(index, away=middle):
        @pl.when(middle)
        def _():
            fourth_out[index].wait_recv()
            fourth_on[index].start()

        @pl.when(away)
        def _():
            fourth_away[index].start()

    def side_take(*some):
        @pl.when(side)
        def _():
            for index in some:
                fourth_away[index].wait_recv()
                fourth_on[index].start()

    def span_of(h, body):
        run([body(h, pair) for pair in range(h * (pairs // 2), (h + 1) * (pairs // 2))])

    to_sibling.wait_recv()
    for h, cols in enumerate(parts):
        span_of(h, first_step)
        if h == 0:
            third_early.wait_recv()
            third_early_on.start()
            sends[4][32:48, :] = halve(blocks[3][pl.ds(mine, 32), :])
            when_start(middle, fourth_out[1])
        second_out[h].wait_recv()
        second_on[h].start()
        sends[3][32:, cols] = halve(blocks[2][pl.ds(mine, HALF), cols])
        third_out[h].start()
        sends[4][16:32, cols] = halve(sends[3][32:, cols])
        when_start(middle, fourth_out[2 + h])
        when_start(has_cross, to_cross[h])
        relay(h)

    to_inner.wait_recv()
    halves(lambda h, pair: tile_step(h, pair, inner_row, [(inner, 0)], False))

    for h, cols in enumerate(parts):
        third_out[h].wait_recv()
        third_on[h].start()
        sends[4][48:, cols] = halve(blocks[3][pl.ds(pl.multiple_of(mine + 32, 32), 32), cols])
        when_start(middle, fourth_out[4 + h])
        relay(2 + h, to_side)

    for copy in second_on + [third_early_on] + third_on:
        copy.wait_recv()
    for h in range(2):
        span_of(h, lambda h, pair: whole_step(h, pair, [(blocks[2], 0), (blocks[3], 0)]))
        relay(4 + h, to_side)
        if h == 0:
            @pl.when(outer)
            def _():
                for index in range(2):
                    fourth_away[index].wait_recv()
                    fourth_on[index].start()

            @pl.when(side)
            def _():
                for index in range(2):
                    fourth_over[index].start()

            side_take(2)

    @pl.when(corner)
    def _():
        for index in range(2):
            fourth_over[index].wait_recv()
            fourth_on[2 + 2 * index].start()
            fourth_on[3 + 2 * index].start()

    side_take(3, 4, 5)

    for level in range(5, levels + 1):
        sends[level][:32, :] = halve(sends[level - 1][...])
        sends[level][32:, :] = halve(blocks[level - 1][pl.ds(mine, HALF), :])
        later_out[level].start()
        later_out[level].wait_recv()
        later_on[level].start()

    for copy in fourth_on + list(later_on.values()):
        copy.wait_recv()
    far = [(blocks[level], 0) for level in range(4, levels + 1)]
    halves(lambda h, pair: tile_step(h, pair, inner_row, far, True))

    @pl.when(has_cross)
    def _():
        for copy in to_cross:
            copy.wait_recv()

    halves(lambda h, pair: tile_step(h, pair, cross_row, far + [(cross, 0)], True))

    w_copy.wait()

    @pl.loop(0, out_ref.shape[1] // 256, unroll=4)
    def _(block):
        cols = pl.ds(pl.multiple_of(block * 256, 256), 256)
        out_ref[:, cols] = jnp.dot(context[...], w_vmem[:, cols],
                                   preferred_element_type=jnp.float32).astype(jnp.bfloat16)

    for copy in [to_sibling, to_inner, third_early, third_early_on] + second_out + second_on + third_out + third_on:
        copy.wait_send()
    for copy in fourth_on + list(later_out.values()) + list(later_on.values()):
        copy.wait_send()

    @pl.when(middle)
    def _():
        for copy in fourth_out + fourth_away[:2]:
            copy.wait_send()

    @pl.when(to_side)
    def _():
        for copy in fourth_away[2:]:
            copy.wait_send()

    @pl.when(side)
    def _():
        for copy in fourth_over:
            copy.wait_send()

    @pl.when(has_cross)
    def _():
        for copy in to_cross:
            copy.wait_send()


def on_device(devices, query_rows, key_rows, value_rows, segment_ids, out_weight):
    tokens, width = query_rows.shape
    levels = devices.bit_length() - 1
    span = 2 * width + LANES
    copies = 34 + 2 * (levels - 4)
    pairs = width // LANES
    bf16 = jnp.bfloat16
    scratch = [
        pltpu.VMEM((tokens, width), bf16),
        pltpu.VMEM((1, tokens), jnp.int32),
        pltpu.SemaphoreType.DMA((6,)),
        pltpu.VMEM((tokens, span), bf16),
        pltpu.VMEM((TILE, span), bf16),
        pltpu.VMEM((TILE, span), bf16),
        pltpu.VMEM((TILE, span), bf16),
        pltpu.VMEM((pairs, 2 * tokens, LANES), bf16),
        pltpu.VMEM((2 * tokens, LANES), bf16),
        pltpu.VMEM((pairs, 2 * tokens, LANES), jnp.float32),
        pltpu.VMEM((pairs, tokens, 2 * LANES), jnp.float32),
        pltpu.VMEM((tokens, width), bf16),
        pltpu.VMEM(out_weight.shape, bf16),
        pltpu.SemaphoreType.DMA,
        pltpu.SemaphoreType.DMA((copies,)),
        pltpu.SemaphoreType.DMA((copies,)),
    ]
    scratch += [pltpu.VMEM((HALF, span), bf16) for _ in range(2, levels + 1)]
    scratch += [pltpu.VMEM((TILE, span), bf16) for _ in range(1, levels + 1)]
    vmem = pl.BlockSpec(memory_space=pltpu.VMEM)
    return pl.pallas_call(
        functools.partial(attend, devices),
        out_shape=jax.ShapeDtypeStruct((tokens, width), bf16),
        in_specs=[pl.BlockSpec(memory_space=pltpu.HBM)] * 5,
        out_specs=vmem,
        scratch_shapes=scratch,
        compiler_params=pltpu.CompilerParams(
            collective_id=0, has_side_effects=True),
    )(query_rows, key_rows, value_rows, segment_ids.reshape(1, tokens), out_weight)


def solution(mesh):
    rows = P(("groups", "seq"), None)
    return jax.shard_map(
        functools.partial(on_device, mesh.shape["seq"]), mesh=mesh,
        in_specs=(rows, rows, rows, P(("groups", "seq")), P()),
        out_specs=rows, check_vma=False)
```

```python
import functools
import jax
import jax.numpy as jnp
from jax import lax
from jax.experimental import pallas as pl
from jax.experimental.pallas import tpu as pltpu
from jax.sharding import PartitionSpec as P

DH = 64
TILE = 128
LANES = 128
HALF = 64
BIG = 2.0**100
MESH = pl.DeviceIdType.MESH


def flip(index, mask):
    bit = 0
    while (1 << bit) <= mask:
        if mask & (1 << bit):
            index = index + (1 - 2 * ((index // (1 << bit)) % 2)) * (1 << bit)
        bit += 1
    return index


def halve(source):
    rows = source.shape[0]
    row = lax.broadcasted_iota(jnp.int32, (rows // 2, rows), 0)
    col = lax.broadcasted_iota(jnp.int32, (rows // 2, rows), 1)
    pick = jnp.where(col // 2 == row, 0.5, 0.0).astype(jnp.bfloat16)
    return jnp.dot(pick, source, preferred_element_type=jnp.float32).astype(jnp.bfloat16)


def attend(devices, q_hbm, k_hbm, v_hbm, seg_hbm, w_hbm, out_ref, q_ref, seg_ref, load_sem, kv, coarse, inner, cross,
           queries, query_seg, largest, total, context, w_vmem, w_sem, send_sem, recv_sem, *rest):
    levels = devices.bit_length() - 1
    sends = dict(zip(range(2, levels + 1), rest))
    blocks = dict(zip(range(1, levels + 1), rest[levels - 1 :]))
    me = lax.axis_index("seq")
    core = me % 2
    tokens, width = q_hbm.shape
    pairs = width // LANES
    part = width // 2
    seg_at = 2 * part
    parts = (slice(0, 2 * part), slice(2 * part, 4 * part + LANES))
    starts = (0, 2 * part + LANES)
    every = slice(0, 4 * part + LANES)
    seg_columns = slice(seg_at, seg_at + LANES)

    middle = (me // 4 + me // 8) % 2 == 1
    outer = jnp.logical_not(middle)
    straight = (me // 2 + me // 4) % 2 == 0
    corner = jnp.logical_and(outer, straight)
    side = jnp.logical_and(outer, jnp.logical_not(straight))
    to_side = jnp.logical_and(middle, straight)
    has_cross = jnp.logical_and(me + core > 0, me + core < devices)
    neighbour = me - 1 + 2 * core
    crooked = (me // 2 + core) % 2 == 0
    near_cross = jnp.logical_and(has_cross, jnp.logical_not(crooked))
    far_cross = jnp.logical_and(has_cross, crooked)
    inner_row = pl.multiple_of((1 - core) * TILE, TILE)
    cross_row = pl.multiple_of(core * TILE, TILE)
    mine = pl.multiple_of(core * HALF, HALF)

    barrier = pltpu.get_barrier_semaphore()
    masks = [1, 2, 4] + [1 << (level - 1) for level in range(5, levels + 1)]
    for mask in masks:
        pl.semaphore_signal(barrier, inc=1, device_id={"seq": flip(me, mask)}, device_id_type=MESH)

    @pl.when(middle)
    def _():
        pl.semaphore_signal(barrier, inc=1, device_id={"seq": flip(me, 12)}, device_id_type=MESH)

    @pl.when(has_cross)
    def _():
        pl.semaphore_signal(barrier, inc=1, device_id={"seq": neighbour}, device_id_type=MESH)

    def load(source, index, from_cols, to_cols):
        return pltpu.make_async_copy(source.at[:, from_cols], kv.at[:, to_cols], load_sem.at[index])

    seg_load = pltpu.make_async_copy(seg_hbm, seg_ref, load_sem.at[0])
    q_load = pltpu.make_async_copy(q_hbm, q_ref, load_sem.at[1])
    loads = []
    for h in range(2):
        base = starts[h]
        loads.append([
            load(k_hbm, 2 + 2 * h, slice(h * part, (h + 1) * part), slice(base, base + part)),
            load(v_hbm, 3 + 2 * h, slice(h * part, (h + 1) * part),
                 slice(base + part, base + 2 * part)),
        ])
    for some in loads:
        for one_load in some:
            one_load.start()
        if some is loads[0]:
            seg_load.start()
    q_load.start()
    made = []

    def remote(source, target, device):
        index = len(made)
        copy = pltpu.make_async_remote_copy(
            src_ref=source, dst_ref=target, send_sem=send_sem.at[index],
            recv_sem=recv_sem.at[index], device_id={"seq": device}, device_id_type=MESH)
        made.append(copy)
        return copy

    def block_part(level, start, rows, cols):
        return blocks[level].at[pl.ds(pl.multiple_of(mine + start, 16), rows), cols]

    def exchange(level, start, rows, cols, mask):
        return remote(sends[level].at[start : start + rows, cols],
                      block_part(level, start, rows, cols), flip(me, mask))

    def forward(level, start, rows, cols, mask=1):
        here = block_part(level, start, rows, cols)
        return remote(here, here, flip(me, mask))

    to_sibling = remote(coarse, blocks[1], flip(me, 1))
    to_inner = remote(kv.at[pl.ds(inner_row, TILE)], inner, flip(me, 1))
    to_cross = [remote(kv.at[pl.ds(cross_row, TILE), cols], cross.at[:, cols], neighbour)
                for cols in parts]
    second_out = [exchange(2, 0, HALF, cols, 2) for cols in parts]
    second_on = [forward(2, 0, HALF, cols) for cols in parts]
    third_early = exchange(3, 0, 32, every, 4)
    third_early_on = forward(3, 0, 32, every)
    third_out = [exchange(3, 32, 32, cols, 4) for cols in parts]
    third_on = [forward(3, 32, 32, cols) for cols in parts]
    pieces = [(0, every), (32, every), (16, parts[0]), (16, parts[1]), (48, parts[0]), (48, parts[1])]
    fourth_out = [exchange(4, start, 16, cols, 12) for start, cols in pieces]
    fourth_on = [forward(4, start, 16, cols) for start, cols in pieces]
    fourth_away = [forward(4, start, 16, cols, 4) for start, cols in pieces]
    fourth_over = [remote(block_part(4, start, 16, every), block_part(4, start + 16, 16, every), flip(me, 2))
                   for start in (0, 32)]
    later_out = {level: exchange(level, 0, HALF, every, 1 << (level - 1))
                 for level in range(5, levels + 1)}
    later_on = {level: forward(level, 0, HALF, every) for level in range(5, levels + 1)}

    def when_start(condition, copy):
        pl.when(condition)(copy.start)

    def set_seg():
        seg_load.wait()

        seg = seg_ref[...]
        first = jnp.sum(jnp.where(seg < 1, 1.0, 0.0), axis=1, keepdims=True)
        second = jnp.sum(jnp.where(seg < 2, 1.0, 0.0), axis=1, keepdims=True)
        row = lax.broadcasted_iota(jnp.int32, (tokens, LANES), 0).astype(jnp.float32)
        lane = lax.broadcasted_iota(jnp.int32, (tokens, LANES), 1).astype(jnp.float32)
        row_seg = jnp.where(row >= first, 1.0, 0.0) + jnp.where(row >= second, 1.0, 0.0)
        kv[:, seg_columns] = jnp.where(lane == row_seg, -BIG, 0.0).astype(jnp.bfloat16)
        other = jnp.where(lane == row_seg, 0.0, jnp.where(lane < 4, 1.0, 0.0)).astype(jnp.bfloat16)
        query_seg[:tokens, :] = other
        query_seg[tokens:, :] = other

    for h, cols in enumerate(parts):
        if h == 1:
            set_seg()
        for one_load in loads[h]:
            one_load.wait()
        coarse[:, cols] = halve(kv[:, cols])
        sends[2][:, cols] = halve(coarse[:, cols])
        if h == 0:
            pl.semaphore_wait(barrier, len(masks) + jnp.where(middle, 1, 0) + jnp.where(has_cross, 1, 0))
        second_out[h].start()
    to_sibling.start()
    to_inner.start()
    sends[3][:32, :] = halve(sends[2][...])
    third_early.start()
    sends[4][:16, :] = halve(sends[3][:32, :])
    when_start(middle, fourth_out[0])

    @pl.when(jnp.logical_not(has_cross))
    def _():
        cross[...] = jnp.zeros(cross.shape, cross.dtype)
        spot = lax.broadcasted_iota(jnp.int32, (TILE, LANES), 1)
        cross[:, seg_columns] = jnp.where(spot == 3, -BIG, 0.0).astype(jnp.bfloat16)

    w_copy = pltpu.make_async_copy(w_hbm, w_vmem, w_sem)
    w_copy.start()
    q_load.wait()

    low_lanes = lax.broadcasted_iota(jnp.int32, (TILE, LANES), 1) < DH
    one = jnp.ones((TILE, LANES), jnp.bfloat16)
    zero = jnp.zeros((TILE, LANES), jnp.bfloat16)
    low_ones = jnp.where(low_lanes, one, zero)
    high_ones = jnp.where(low_lanes, zero, one)

    def columns(h, pair):
        at = starts[h] + (pair - h * (pairs // 2)) * LANES
        return (pl.ds(pl.multiple_of(at, LANES), LANES),
                pl.ds(pl.multiple_of(at + part, LANES), LANES))

    def score(left_side, spots, key_cols):
        right_side = jnp.concatenate(
            [jnp.concatenate([ref[base : base + TILE, key_cols], ref[base : base + TILE, seg_columns]],
                             axis=1) for ref, base in spots], axis=0)
        return lax.dot_general(left_side, right_side, (((1,), (1,)), ((), ())),
                               preferred_element_type=jnp.float32)

    def highest(scores):
        top = scores[:, :LANES]
        for at in range(LANES, scores.shape[1], LANES):
            top = jnp.maximum(top, scores[:, at : at + LANES])
        return jnp.broadcast_to(jnp.max(top, axis=1, keepdims=True), top.shape)

    def weigh(scores, top, spots, value_cols):
        half = top.shape[0] // 2
        left_side, right_side = [], []
        for index, (ref, base) in enumerate(spots):
            some = scores[:, index * LANES : (index + 1) * LANES]
            weights = jnp.exp(some - top).astype(jnp.bfloat16)
            values = ref[base : base + TILE, value_cols]
            left_side += [weights[:half], weights[half:]]
            right_side += [
                jnp.concatenate([jnp.where(low_lanes, values, zero), low_ones], axis=1),
                jnp.concatenate([jnp.where(low_lanes, zero, values), high_ones], axis=1),
            ]
        return jnp.dot(jnp.concatenate(left_side, axis=1), jnp.concatenate(right_side, axis=0),
                       preferred_element_type=jnp.float32)

    def rescale(old, top):
        shrink = jnp.exp(old - top)
        half = top.shape[0] // 2
        lanes = lax.broadcasted_iota(jnp.int32, (half, LANES), 1) < DH
        both = jnp.where(lanes, shrink[:half], shrink[half:])
        return jnp.concatenate([both, both], axis=1)

    def whole_step(h, pair, spots):
        key_cols, value_cols = columns(h, pair)
        left_side = jnp.concatenate([queries[pair], query_seg[...]], axis=1)
        scores = score(left_side, spots, key_cols)
        yield
        old = largest[pair]
        top = jnp.maximum(old, highest(scores))
        yield
        largest[pair] = top
        total[pair] = total[pair] * rescale(old, top) + weigh(scores, top, spots, value_cols)

    def tile_step(h, pair, start, spots, last):
        key_cols, value_cols = columns(h, pair)
        heads = (pl.ds(start, TILE), pl.ds(pl.multiple_of(start + tokens, TILE), TILE))
        left_side = jnp.concatenate(
            [jnp.concatenate([queries[pair, head], query_seg[head, :]], axis=1) for head in heads], axis=0)
        scores = score(left_side, spots, key_cols)
        yield
        old = jnp.concatenate([largest[pair, head] for head in heads], axis=0)
        top = jnp.maximum(old, highest(scores))
        yield
        acc = total[pair, heads[0]] * rescale(old, top) + weigh(scores, top, spots, value_cols)
        if last:
            context[heads[0], pl.ds(pl.multiple_of(pair * LANES, LANES), LANES)] = (
                acc[:, :LANES] / acc[:, LANES:]).astype(jnp.bfloat16)
        else:
            for index, head in enumerate(heads):
                largest[pair, head] = top[index * TILE : (index + 1) * TILE]
            total[pair, heads[0]] = acc

    def run(steps):
        for _ in range(3):
            for step in steps:
                next(step, None)

    def halves(body):
        run([body(pair // (pairs // 2), pair) for pair in range(pairs)])

    near = [(kv, 0), (kv, TILE), (blocks[1], 0)]

    def first_step(h, pair):
        key_cols, value_cols = columns(h, pair)
        scaled = q_ref[:, pl.ds(pl.multiple_of(pair * LANES, LANES), LANES)] * jnp.bfloat16(DH**-0.5)
        lanes = lax.broadcasted_iota(jnp.int32, (tokens, LANES), 1) < DH
        none = jnp.zeros_like(scaled)
        both = jnp.concatenate([jnp.where(lanes, scaled, none), jnp.where(lanes, none, scaled)], axis=0)
        queries[pair] = both
        scores = score(jnp.concatenate([both, query_seg[...]], axis=1), near, key_cols)
        yield
        top = highest(scores)
        yield
        largest[pair] = top
        total[pair] = weigh(scores, top, near, value_cols)

    def relay(index, away=middle):
        @pl.when(middle)
        def _():
            fourth_out[index].wait_recv()
            fourth_on[index].start()

        @pl.when(away)
        def _():
            fourth_away[index].start()

    def outer_take(index):
        @pl.when(outer)
        def _():
            fourth_away[index].wait_recv()
            fourth_on[index].start()

        when_start(side, fourth_over[index])

    def side_take(*some):
        @pl.when(side)
        def _():
            for index in some:
                fourth_away[index].wait_recv()
                fourth_on[index].start()

    def span_of(h, body):
        run([body(h, pair) for pair in range(h * (pairs // 2), (h + 1) * (pairs // 2))])

    to_sibling.wait_recv()
    for h, cols in enumerate(parts):
        span_of(h, first_step)
        if h == 0:
            third_early.wait_recv()
            third_early_on.start()
            sends[4][32:48, :] = halve(blocks[3][pl.ds(mine, 32), :])
            when_start(middle, fourth_out[1])
        second_out[h].wait_recv()
        second_on[h].start()
        sends[3][32:, cols] = halve(blocks[2][pl.ds(mine, HALF), cols])
        third_out[h].start()
        sends[4][16:32, cols] = halve(sends[3][32:, cols])
        when_start(middle, fourth_out[2 + h])
        when_start(near_cross, to_cross[h])
        relay(h)

    to_inner.wait_recv()
    halves(lambda h, pair: tile_step(h, pair, inner_row, [(inner, 0)], False))

    for copy in to_cross:
        when_start(far_cross, copy)
    outer_take(0)
    for h, cols in enumerate(parts):
        third_out[h].wait_recv()
        third_on[h].start()
        sends[4][48:, cols] = halve(blocks[3][pl.ds(pl.multiple_of(mine + 32, 32), 32), cols])
        when_start(middle, fourth_out[4 + h])
        relay(2 + h, to_side)
        if h == 0:
            outer_take(1)

    for copy in second_on + [third_early_on] + third_on:
        copy.wait_recv()
    for h in range(2):
        span_of(h, lambda h, pair: whole_step(h, pair, [(blocks[2], 0), (blocks[3], 0)]))
        relay(4 + h, to_side)
        if h == 0:
            side_take(2)

    @pl.when(corner)
    def _():
        for index in range(2):
            fourth_over[index].wait_recv()
            fourth_on[2 + 2 * index].start()
            fourth_on[3 + 2 * index].start()

    side_take(3, 4, 5)

    for level in range(5, levels + 1):
        sends[level][:32, :] = halve(sends[level - 1][...])
        sends[level][32:, :] = halve(blocks[level - 1][pl.ds(mine, HALF), :])
        later_out[level].start()
        later_out[level].wait_recv()
        later_on[level].start()

    for copy in fourth_on + list(later_on.values()):
        copy.wait_recv()
    far = [(blocks[level], 0) for level in range(4, levels + 1)]
    halves(lambda h, pair: tile_step(h, pair, inner_row, far, True))

    @pl.when(has_cross)
    def _():
        for copy in to_cross:
            copy.wait_recv()

    halves(lambda h, pair: tile_step(h, pair, cross_row, far + [(cross, 0)], True))

    w_copy.wait()

    @pl.loop(0, out_ref.shape[1] // 256, unroll=4)
    def _(block):
        cols = pl.ds(pl.multiple_of(block * 256, 256), 256)
        out_ref[:, cols] = jnp.dot(context[...], w_vmem[:, cols],
                                   preferred_element_type=jnp.float32).astype(jnp.bfloat16)

    for copy in [to_sibling, to_inner, third_early, third_early_on] + second_out + second_on + third_out + third_on:
        copy.wait_send()
    for copy in fourth_on + list(later_out.values()) + list(later_on.values()):
        copy.wait_send()

    @pl.when(middle)
    def _():
        for copy in fourth_out + fourth_away[:2]:
            copy.wait_send()

    @pl.when(to_side)
    def _():
        for copy in fourth_away[2:]:
            copy.wait_send()

    @pl.when(side)
    def _():
        for copy in fourth_over:
            copy.wait_send()

    @pl.when(has_cross)
    def _():
        for copy in to_cross:
            copy.wait_send()


def on_device(devices, query_rows, key_rows, value_rows, segment_ids, out_weight):
    tokens, width = query_rows.shape
    levels = devices.bit_length() - 1
    span = 2 * width + LANES
    copies = 34 + 2 * (levels - 4)
    pairs = width // LANES
    bf16 = jnp.bfloat16
    scratch = [
        pltpu.VMEM((tokens, width), bf16),
        pltpu.VMEM((1, tokens), jnp.int32),
        pltpu.SemaphoreType.DMA((6,)),
        pltpu.VMEM((tokens, span), bf16),
        pltpu.VMEM((TILE, span), bf16),
        pltpu.VMEM((TILE, span), bf16),
        pltpu.VMEM((TILE, span), bf16),
        pltpu.VMEM((pairs, 2 * tokens, LANES), bf16),
        pltpu.VMEM((2 * tokens, LANES), bf16),
        pltpu.VMEM((pairs, 2 * tokens, LANES), jnp.float32),
        pltpu.VMEM((pairs, tokens, 2 * LANES), jnp.float32),
        pltpu.VMEM((tokens, width), bf16),
        pltpu.VMEM(out_weight.shape, bf16),
        pltpu.SemaphoreType.DMA,
        pltpu.SemaphoreType.DMA((copies,)),
        pltpu.SemaphoreType.DMA((copies,)),
    ]
    scratch += [pltpu.VMEM((HALF, span), bf16) for _ in range(2, levels + 1)]
    scratch += [pltpu.VMEM((TILE, span), bf16) for _ in range(1, levels + 1)]
    vmem = pl.BlockSpec(memory_space=pltpu.VMEM)
    return pl.pallas_call(
        functools.partial(attend, devices),
        out_shape=jax.ShapeDtypeStruct((tokens, width), bf16),
        in_specs=[pl.BlockSpec(memory_space=pltpu.HBM)] * 5,
        out_specs=vmem,
        scratch_shapes=scratch,
        compiler_params=pltpu.CompilerParams(
            collective_id=0, has_side_effects=True),
    )(query_rows, key_rows, value_rows, segment_ids.reshape(1, tokens), out_weight)


def solution(mesh):
    rows = P(("groups", "seq"), None)
    return jax.shard_map(
        functools.partial(on_device, mesh.shape["seq"]), mesh=mesh,
        in_specs=(rows, rows, rows, P(("groups", "seq")), P()),
        out_specs=rows, check_vma=False)
```

```python
import functools
import jax
import jax.numpy as jnp
from jax import lax
from jax.experimental import pallas as pl
from jax.experimental.pallas import tpu as pltpu
from jax.sharding import PartitionSpec as P

DH = 64
TILE = 128
LANES = 128
HALF = 64
BIG = 2.0**100
MESH = pl.DeviceIdType.MESH


def flip(index, mask):
    bit = 0
    while (1 << bit) <= mask:
        if mask & (1 << bit):
            index = index + (1 - 2 * ((index // (1 << bit)) % 2)) * (1 << bit)
        bit += 1
    return index


def halve(source):
    rows = source.shape[0]
    row = lax.broadcasted_iota(jnp.int32, (rows // 2, rows), 0)
    col = lax.broadcasted_iota(jnp.int32, (rows // 2, rows), 1)
    pick = jnp.where(col // 2 == row, 0.5, 0.0).astype(jnp.bfloat16)
    return jnp.dot(pick, source, preferred_element_type=jnp.float32).astype(jnp.bfloat16)


def attend(devices, q_hbm, k_hbm, v_hbm, seg_hbm, w_hbm, out_ref, q_ref, seg_ref, load_sem, kv, coarse, inner, cross,
           queries, query_seg, largest, total, context, w_vmem, w_sem, send_sem, recv_sem, count_out, count_in,
           *rest):
    levels = devices.bit_length() - 1
    sends = dict(zip(range(2, levels + 1), rest))
    blocks = dict(zip(range(1, levels + 1), rest[levels - 1 :]))
    me = lax.axis_index("seq")
    core = me % 2
    tokens, width = q_hbm.shape
    pairs = width // LANES
    part = width // 2
    seg_at = 2 * part
    parts = (slice(0, 2 * part), slice(2 * part, 4 * part + LANES))
    starts = (0, 2 * part + LANES)
    every = slice(0, 4 * part + LANES)
    seg_columns = slice(seg_at, seg_at + LANES)

    middle = (me // 4 + me // 8) % 2 == 1
    outer = jnp.logical_not(middle)
    straight = (me // 2 + me // 4) % 2 == 0
    corner = jnp.logical_and(outer, straight)
    lag = middle
    side = jnp.logical_and(outer, jnp.logical_not(straight))
    to_side = jnp.logical_and(middle, straight)
    has_cross = jnp.logical_and(me + core > 0, me + core < devices)
    neighbour = me - 1 + 2 * core
    crooked = (me // 2 + core) % 2 == 0
    near_cross = jnp.logical_and(has_cross, jnp.logical_not(crooked))
    far_cross = jnp.logical_and(has_cross, crooked)
    soon_cross = jnp.logical_and(far_cross, jnp.logical_not(lag))
    late_cross = jnp.logical_and(far_cross, lag)
    inner_row = pl.multiple_of((1 - core) * TILE, TILE)
    cross_row = pl.multiple_of(core * TILE, TILE)
    mine = pl.multiple_of(core * HALF, HALF)

    barrier = pltpu.get_barrier_semaphore()
    masks = [1, 2, 4] + [1 << (level - 1) for level in range(5, levels + 1)]
    for mask in masks:
        pl.semaphore_signal(barrier, inc=1, device_id={"seq": flip(me, mask)}, device_id_type=MESH)

    @pl.when(middle)
    def _():
        pl.semaphore_signal(barrier, inc=1, device_id={"seq": flip(me, 12)}, device_id_type=MESH)

    @pl.when(has_cross)
    def _():
        pl.semaphore_signal(barrier, inc=1, device_id={"seq": neighbour}, device_id_type=MESH)

    def load(source, index, from_cols, to_cols):
        return pltpu.make_async_copy(source.at[:, from_cols], kv.at[:, to_cols], load_sem.at[index])

    seg_load = pltpu.make_async_copy(seg_hbm, seg_ref, load_sem.at[0])
    q_load = pltpu.make_async_copy(q_hbm, q_ref, load_sem.at[1])
    loads = []
    for h in range(2):
        base = starts[h]
        loads.append([
            load(k_hbm, 2 + 2 * h, slice(h * part, (h + 1) * part), slice(base, base + part)),
            load(v_hbm, 3 + 2 * h, slice(h * part, (h + 1) * part),
                 slice(base + part, base + 2 * part)),
        ])
    for some in loads:
        for one_load in some:
            one_load.start()
        if some is loads[0]:
            seg_load.start()
    q_load.start()
    made = []

    def remote(source, target, device):
        index = len(made)
        copy = pltpu.make_async_remote_copy(
            src_ref=source, dst_ref=target, send_sem=send_sem.at[index],
            recv_sem=recv_sem.at[index], device_id={"seq": device}, device_id_type=MESH)
        made.append(copy)
        return copy

    def block_part(level, start, rows, cols):
        return blocks[level].at[pl.ds(pl.multiple_of(mine + start, 16), rows), cols]

    def exchange(level, start, rows, cols, mask):
        return remote(sends[level].at[start : start + rows, cols],
                      block_part(level, start, rows, cols), flip(me, mask))

    def forward(level, start, rows, cols, mask=1):
        here = block_part(level, start, rows, cols)
        return remote(here, here, flip(me, mask))

    to_sibling = remote(coarse, blocks[1], flip(me, 1))
    to_inner = remote(kv.at[pl.ds(inner_row, TILE)], inner, flip(me, 1))
    to_cross = [remote(kv.at[pl.ds(cross_row, TILE), cols], cross.at[:, cols], neighbour)
                for cols in (parts[0], slice(starts[1], starts[1] + 2 * part))]
    count_cross = remote(count_out, count_in, neighbour)
    second_out = [exchange(2, 0, HALF, cols, 2) for cols in parts]
    second_on = [forward(2, 0, HALF, cols) for cols in parts]
    third_early = exchange(3, 0, 32, every, 4)
    third_early_on = forward(3, 0, 32, every)
    third_out = [exchange(3, 32, 32, cols, 4) for cols in parts]
    third_on = [forward(3, 32, 32, cols) for cols in parts]
    pieces = [(0, every), (32, every), (16, parts[0]), (16, parts[1]), (48, parts[0]), (48, parts[1])]
    fourth_out = [exchange(4, start, 16, cols, 12) for start, cols in pieces]
    fourth_on = [forward(4, start, 16, cols) for start, cols in pieces]
    fourth_away = [forward(4, start, 16, cols, 4) for start, cols in pieces]
    fourth_over = [remote(block_part(4, start, 16, every), block_part(4, start + 16, 16, every), flip(me, 2))
                   for start in (0, 32)]
    later_out = {level: exchange(level, 0, HALF, every, 1 << (level - 1))
                 for level in range(5, levels + 1)}
    later_on = {level: forward(level, 0, HALF, every) for level in range(5, levels + 1)}

    def when_start(condition, copy):
        pl.when(condition)(copy.start)

    def set_seg():
        seg_load.wait()

        seg = seg_ref[...]
        first = jnp.sum(jnp.where(seg < 1, 1.0, 0.0), axis=1, keepdims=True)
        second = jnp.sum(jnp.where(seg < 2, 1.0, 0.0), axis=1, keepdims=True)
        spot = lax.broadcasted_iota(jnp.int32, (8, LANES), 0)
        count_out[...] = jnp.where(spot == 0, first, second)
        row = lax.broadcasted_iota(jnp.int32, (tokens, LANES), 0).astype(jnp.float32)
        lane = lax.broadcasted_iota(jnp.int32, (tokens, LANES), 1).astype(jnp.float32)
        row_seg = jnp.where(row >= first, 1.0, 0.0) + jnp.where(row >= second, 1.0, 0.0)
        kv[:, seg_columns] = jnp.where(lane == row_seg, -BIG, 0.0).astype(jnp.bfloat16)
        other = jnp.where(lane == row_seg, 0.0, jnp.where(lane < 4, 1.0, 0.0)).astype(jnp.bfloat16)
        query_seg[:tokens, :] = other
        query_seg[tokens:, :] = other

    for h, cols in enumerate(parts):
        if h == 1:
            set_seg()
        for one_load in loads[h]:
            one_load.wait()
        coarse[:, cols] = halve(kv[:, cols])
        sends[2][:, cols] = halve(coarse[:, cols])
        if h == 0:
            pl.semaphore_wait(barrier, len(masks) + jnp.where(middle, 1, 0) + jnp.where(has_cross, 1, 0))
        second_out[h].start()
    to_sibling.start()
    to_inner.start()
    when_start(has_cross, count_cross)
    sends[3][:32, :] = halve(sends[2][...])
    third_early.start()
    sends[4][:16, :] = halve(sends[3][:32, :])
    when_start(middle, fourth_out[0])

    @pl.when(jnp.logical_not(has_cross))
    def _():
        cross[...] = jnp.zeros(cross.shape, cross.dtype)
        spot = lax.broadcasted_iota(jnp.int32, (TILE, LANES), 1)
        cross[:, seg_columns] = jnp.where(spot == 3, -BIG, 0.0).astype(jnp.bfloat16)

    w_copy = pltpu.make_async_copy(w_hbm, w_vmem, w_sem)
    w_copy.start()
    q_load.wait()

    low_lanes = lax.broadcasted_iota(jnp.int32, (TILE, LANES), 1) < DH
    one = jnp.ones((TILE, LANES), jnp.bfloat16)
    zero = jnp.zeros((TILE, LANES), jnp.bfloat16)
    low_ones = jnp.where(low_lanes, one, zero)
    high_ones = jnp.where(low_lanes, zero, one)

    def columns(h, pair):
        at = starts[h] + (pair - h * (pairs // 2)) * LANES
        return (pl.ds(pl.multiple_of(at, LANES), LANES),
                pl.ds(pl.multiple_of(at + part, LANES), LANES))

    def score(left_side, spots, key_cols):
        right_side = jnp.concatenate(
            [jnp.concatenate([ref[base : base + TILE, key_cols], ref[base : base + TILE, seg_columns]],
                             axis=1) for ref, base in spots], axis=0)
        return lax.dot_general(left_side, right_side, (((1,), (1,)), ((), ())),
                               preferred_element_type=jnp.float32)

    def highest(scores):
        top = scores[:, :LANES]
        for at in range(LANES, scores.shape[1], LANES):
            top = jnp.maximum(top, scores[:, at : at + LANES])
        return jnp.broadcast_to(jnp.max(top, axis=1, keepdims=True), top.shape)

    def weigh(scores, top, spots, value_cols):
        half = top.shape[0] // 2
        left_side, right_side = [], []
        for index, (ref, base) in enumerate(spots):
            some = scores[:, index * LANES : (index + 1) * LANES]
            weights = jnp.exp(some - top).astype(jnp.bfloat16)
            values = ref[base : base + TILE, value_cols]
            left_side += [weights[:half], weights[half:]]
            right_side += [
                jnp.concatenate([jnp.where(low_lanes, values, zero), low_ones], axis=1),
                jnp.concatenate([jnp.where(low_lanes, zero, values), high_ones], axis=1),
            ]
        return jnp.dot(jnp.concatenate(left_side, axis=1), jnp.concatenate(right_side, axis=0),
                       preferred_element_type=jnp.float32)

    def rescale(old, top):
        shrink = jnp.exp(old - top)
        half = top.shape[0] // 2
        lanes = lax.broadcasted_iota(jnp.int32, (half, LANES), 1) < DH
        both = jnp.where(lanes, shrink[:half], shrink[half:])
        return jnp.concatenate([both, both], axis=1)

    def whole_step(h, pair, spots):
        key_cols, value_cols = columns(h, pair)
        left_side = jnp.concatenate([queries[pair], query_seg[...]], axis=1)
        scores = score(left_side, spots, key_cols)
        yield
        old = largest[pair]
        top = jnp.maximum(old, highest(scores))
        yield
        largest[pair] = top
        total[pair] = total[pair] * rescale(old, top) + weigh(scores, top, spots, value_cols)

    def tile_step(h, pair, start, spots, last):
        key_cols, value_cols = columns(h, pair)
        heads = (pl.ds(start, TILE), pl.ds(pl.multiple_of(start + tokens, TILE), TILE))
        left_side = jnp.concatenate(
            [jnp.concatenate([queries[pair, head], query_seg[head, :]], axis=1) for head in heads], axis=0)
        scores = score(left_side, spots, key_cols)
        yield
        old = jnp.concatenate([largest[pair, head] for head in heads], axis=0)
        top = jnp.maximum(old, highest(scores))
        yield
        acc = total[pair, heads[0]] * rescale(old, top) + weigh(scores, top, spots, value_cols)
        if last:
            context[heads[0], pl.ds(pl.multiple_of(pair * LANES, LANES), LANES)] = (
                acc[:, :LANES] / acc[:, LANES:]).astype(jnp.bfloat16)
        else:
            for index, head in enumerate(heads):
                largest[pair, head] = top[index * TILE : (index + 1) * TILE]
            total[pair, heads[0]] = acc

    def run(steps):
        for _ in range(3):
            for step in steps:
                next(step, None)

    def halves(body):
        run([body(pair // (pairs // 2), pair) for pair in range(pairs)])

    near = [(kv, 0), (kv, TILE), (blocks[1], 0)]

    def first_step(h, pair):
        key_cols, value_cols = columns(h, pair)
        scaled = q_ref[:, pl.ds(pl.multiple_of(pair * LANES, LANES), LANES)] * jnp.bfloat16(DH**-0.5)
        lanes = lax.broadcasted_iota(jnp.int32, (tokens, LANES), 1) < DH
        none = jnp.zeros_like(scaled)
        both = jnp.concatenate([jnp.where(lanes, scaled, none), jnp.where(lanes, none, scaled)], axis=0)
        queries[pair] = both
        scores = score(jnp.concatenate([both, query_seg[...]], axis=1), near, key_cols)
        yield
        top = highest(scores)
        yield
        largest[pair] = top
        total[pair] = weigh(scores, top, near, value_cols)

    def relay(index, away=middle):
        @pl.when(middle)
        def _():
            fourth_out[index].wait_recv()
            fourth_on[index].start()

        @pl.when(away)
        def _():
            fourth_away[index].start()

    def outer_take(index):
        @pl.when(outer)
        def _():
            fourth_away[index].wait_recv()
            fourth_on[index].start()

        when_start(side, fourth_over[index])

    def side_take(*some):
        @pl.when(side)
        def _():
            for index in some:
                fourth_away[index].wait_recv()
                fourth_on[index].start()

    def span_of(h, body):
        run([body(h, pair) for pair in range(h * (pairs // 2), (h + 1) * (pairs // 2))])

    to_sibling.wait_recv()
    for h, cols in enumerate(parts):
        span_of(h, first_step)
        if h == 0:
            third_early.wait_recv()
            third_early_on.start()
            sends[4][32:48, :] = halve(blocks[3][pl.ds(mine, 32), :])
            when_start(middle, fourth_out[1])
        second_out[h].wait_recv()
        second_on[h].start()
        sends[3][32:, cols] = halve(blocks[2][pl.ds(mine, HALF), cols])
        third_out[h].start()
        sends[4][16:32, cols] = halve(sends[3][32:, cols])
        when_start(middle, fourth_out[2 + h])
        if h == 0:
            for copy in to_cross:
                when_start(near_cross, copy)
        relay(h)

    to_inner.wait_recv()
    halves(lambda h, pair: tile_step(h, pair, inner_row, [(inner, 0)], False))

    for copy in to_cross:
        when_start(soon_cross, copy)
    outer_take(0)
    for h, cols in enumerate(parts):
        third_out[h].wait_recv()
        third_on[h].start()
        sends[4][48:, cols] = halve(blocks[3][pl.ds(pl.multiple_of(mine + 32, 32), 32), cols])
        when_start(middle, fourth_out[4 + h])
        relay(2 + h, to_side)
        when_start(late_cross, to_cross[h])
        if h == 0:
            outer_take(1)

    @pl.when(has_cross)
    def _():
        count_cross.wait_recv()
        row = (lax.broadcasted_iota(jnp.int32, (TILE, LANES), 0) + inner_row).astype(jnp.float32)
        lane = lax.broadcasted_iota(jnp.int32, (TILE, LANES), 1).astype(jnp.float32)
        kind = jnp.where(row >= count_in[0:1, :], 1.0, 0.0) + jnp.where(row >= count_in[1:2, :], 1.0, 0.0)
        cross[:, seg_columns] = jnp.where(lane == kind, -BIG, 0.0).astype(jnp.bfloat16)

    for copy in second_on + [third_early_on] + third_on:
        copy.wait_recv()
    for h in range(2):
        span_of(h, lambda h, pair: whole_step(h, pair, [(blocks[2], 0), (blocks[3], 0)]))
        relay(4 + h, to_side)
        if h == 0:
            side_take(2)

    @pl.when(corner)
    def _():
        for index in range(2):
            fourth_over[index].wait_recv()
            fourth_on[2 + 2 * index].start()
            fourth_on[3 + 2 * index].start()

    side_take(3, 4, 5)

    for level in range(5, levels + 1):
        sends[level][:32, :] = halve(sends[level - 1][...])
        sends[level][32:, :] = halve(blocks[level - 1][pl.ds(mine, HALF), :])
        later_out[level].start()
        later_out[level].wait_recv()
        later_on[level].start()

    for copy in fourth_on + list(later_on.values()):
        copy.wait_recv()
    far = [(blocks[level], 0) for level in range(4, levels + 1)]
    halves(lambda h, pair: tile_step(h, pair, inner_row, far, True))

    @pl.when(has_cross)
    def _():
        for copy in to_cross:
            copy.wait_recv()

    halves(lambda h, pair: tile_step(h, pair, cross_row, far + [(cross, 0)], True))

    w_copy.wait()

    @pl.loop(0, out_ref.shape[1] // 256, unroll=4)
    def _(block):
        cols = pl.ds(pl.multiple_of(block * 256, 256), 256)
        out_ref[:, cols] = jnp.dot(context[...], w_vmem[:, cols],
                                   preferred_element_type=jnp.float32).astype(jnp.bfloat16)

    for copy in [to_sibling, to_inner, third_early, third_early_on] + second_out + second_on + third_out + third_on:
        copy.wait_send()
    for copy in fourth_on + list(later_out.values()) + list(later_on.values()):
        copy.wait_send()

    @pl.when(middle)
    def _():
        for copy in fourth_out + fourth_away[:2]:
            copy.wait_send()

    @pl.when(to_side)
    def _():
        for copy in fourth_away[2:]:
            copy.wait_send()

    @pl.when(side)
    def _():
        for copy in fourth_over:
            copy.wait_send()

    @pl.when(has_cross)
    def _():
        for copy in to_cross + [count_cross]:
            copy.wait_send()


def on_device(devices, query_rows, key_rows, value_rows, segment_ids, out_weight):
    tokens, width = query_rows.shape
    levels = devices.bit_length() - 1
    span = 2 * width + LANES
    copies = 35 + 2 * (levels - 4)
    pairs = width // LANES
    bf16 = jnp.bfloat16
    scratch = [
        pltpu.VMEM((tokens, width), bf16),
        pltpu.VMEM((1, tokens), jnp.int32),
        pltpu.SemaphoreType.DMA((6,)),
        pltpu.VMEM((tokens, span), bf16),
        pltpu.VMEM((TILE, span), bf16),
        pltpu.VMEM((TILE, span), bf16),
        pltpu.VMEM((TILE, span), bf16),
        pltpu.VMEM((pairs, 2 * tokens, LANES), bf16),
        pltpu.VMEM((2 * tokens, LANES), bf16),
        pltpu.VMEM((pairs, 2 * tokens, LANES), jnp.float32),
        pltpu.VMEM((pairs, tokens, 2 * LANES), jnp.float32),
        pltpu.VMEM((tokens, width), bf16),
        pltpu.VMEM(out_weight.shape, bf16),
        pltpu.SemaphoreType.DMA,
        pltpu.SemaphoreType.DMA((copies,)),
        pltpu.SemaphoreType.DMA((copies,)),
        pltpu.VMEM((8, LANES), jnp.float32),
        pltpu.VMEM((8, LANES), jnp.float32),
    ]
    scratch += [pltpu.VMEM((HALF, span), bf16) for _ in range(2, levels + 1)]
    scratch += [pltpu.VMEM((TILE, span), bf16) for _ in range(1, levels + 1)]
    vmem = pl.BlockSpec(memory_space=pltpu.VMEM)
    return pl.pallas_call(
        functools.partial(attend, devices),
        out_shape=jax.ShapeDtypeStruct((tokens, width), bf16),
        in_specs=[pl.BlockSpec(memory_space=pltpu.HBM)] * 5,
        out_specs=vmem,
        scratch_shapes=scratch,
        compiler_params=pltpu.CompilerParams(
            collective_id=0, has_side_effects=True),
    )(query_rows, key_rows, value_rows, segment_ids.reshape(1, tokens), out_weight)


def solution(mesh):
    rows = P(("groups", "seq"), None)
    return jax.shard_map(
        functools.partial(on_device, mesh.shape["seq"]), mesh=mesh,
        in_specs=(rows, rows, rows, P(("groups", "seq")), P()),
        out_specs=rows, check_vma=False)
```

```python
import functools
import jax
import jax.numpy as jnp
from jax import lax
from jax.experimental import pallas as pl
from jax.experimental.pallas import tpu as pltpu
from jax.sharding import PartitionSpec as P

DH = 64
TILE = 128
LANES = 128
HALF = 64
BIG = 2.0**100
MESH = pl.DeviceIdType.MESH


def flip(index, mask):
    bit = 0
    while (1 << bit) <= mask:
        if mask & (1 << bit):
            index = index + (1 - 2 * ((index // (1 << bit)) % 2)) * (1 << bit)
        bit += 1
    return index


def halve(source):
    rows = source.shape[0]
    row = lax.broadcasted_iota(jnp.int32, (rows // 2, rows), 0)
    col = lax.broadcasted_iota(jnp.int32, (rows // 2, rows), 1)
    pick = jnp.where(col // 2 == row, 0.5, 0.0).astype(jnp.bfloat16)
    return jnp.dot(pick, source, preferred_element_type=jnp.float32).astype(jnp.bfloat16)


def attend(devices, q_hbm, k_hbm, v_hbm, seg_hbm, w_hbm, out_ref, q_ref, seg_ref, load_sem, kv, coarse, inner, cross,
           queries, query_seg, largest, total, context, w_vmem, w_sem, send_sem, recv_sem, count_out, count_in,
           *rest):
    levels = devices.bit_length() - 1
    sends = dict(zip(range(2, levels + 1), rest))
    blocks = dict(zip(range(1, levels + 1), rest[levels - 1 :]))
    me = lax.axis_index("seq")
    core = me % 2
    tokens, width = q_hbm.shape
    pairs = width // LANES
    part = width // 2
    seg_at = 2 * part
    parts = (slice(0, 2 * part), slice(2 * part, 4 * part + LANES))
    starts = (0, 2 * part + LANES)
    every = slice(0, 4 * part + LANES)
    seg_columns = slice(seg_at, seg_at + LANES)

    middle = (me // 4 + me // 8) % 2 == 1
    outer = jnp.logical_not(middle)
    straight = (me // 2 + me // 4) % 2 == 0
    corner = jnp.logical_and(outer, straight)
    lag = middle
    side = jnp.logical_and(outer, jnp.logical_not(straight))
    to_side = jnp.logical_and(middle, straight)
    has_cross = jnp.logical_and(me + core > 0, me + core < devices)
    neighbour = me - 1 + 2 * core
    crooked = (me // 2 + core) % 2 == 0
    near_cross = jnp.logical_and(has_cross, jnp.logical_not(crooked))
    far_cross = jnp.logical_and(has_cross, crooked)
    soon_cross = jnp.logical_and(far_cross, jnp.logical_not(lag))
    late_cross = jnp.logical_and(far_cross, lag)
    inner_row = pl.multiple_of((1 - core) * TILE, TILE)
    cross_row = pl.multiple_of(core * TILE, TILE)
    mine = pl.multiple_of(core * HALF, HALF)

    barrier = pltpu.get_barrier_semaphore()
    masks = [1, 2, 4] + [1 << (level - 1) for level in range(5, levels + 1)]
    for mask in masks:
        pl.semaphore_signal(barrier, inc=1, device_id={"seq": flip(me, mask)}, device_id_type=MESH)

    @pl.when(middle)
    def _():
        pl.semaphore_signal(barrier, inc=1, device_id={"seq": flip(me, 12)}, device_id_type=MESH)

    @pl.when(has_cross)
    def _():
        pl.semaphore_signal(barrier, inc=1, device_id={"seq": neighbour}, device_id_type=MESH)

    def load(source, index, from_cols, to_cols):
        return pltpu.make_async_copy(source.at[:, from_cols], kv.at[:, to_cols], load_sem.at[index])

    seg_load = pltpu.make_async_copy(seg_hbm, seg_ref, load_sem.at[0])
    q_load = pltpu.make_async_copy(q_hbm, q_ref, load_sem.at[1])
    loads = []
    for h in range(2):
        base = starts[h]
        loads.append([
            load(k_hbm, 2 + 2 * h, slice(h * part, (h + 1) * part), slice(base, base + part)),
            load(v_hbm, 3 + 2 * h, slice(h * part, (h + 1) * part),
                 slice(base + part, base + 2 * part)),
        ])
    for some in loads:
        for one_load in some:
            one_load.start()
        if some is loads[0]:
            seg_load.start()
    q_load.start()
    made = []

    def remote(source, target, device):
        index = len(made)
        copy = pltpu.make_async_remote_copy(
            src_ref=source, dst_ref=target, send_sem=send_sem.at[index],
            recv_sem=recv_sem.at[index], device_id={"seq": device}, device_id_type=MESH)
        made.append(copy)
        return copy

    def block_part(level, start, rows, cols):
        return blocks[level].at[pl.ds(pl.multiple_of(mine + start, 16), rows), cols]

    def exchange(level, start, rows, cols, mask):
        return remote(sends[level].at[start : start + rows, cols],
                      block_part(level, start, rows, cols), flip(me, mask))

    def forward(level, start, rows, cols, mask=1):
        here = block_part(level, start, rows, cols)
        return remote(here, here, flip(me, mask))

    to_sibling = remote(coarse, blocks[1], flip(me, 1))
    to_inner = remote(kv.at[pl.ds(inner_row, TILE)], inner, flip(me, 1))
    to_cross = [remote(kv.at[pl.ds(cross_row, TILE), cols], cross.at[:, cols], neighbour)
                for cols in (parts[0], slice(starts[1], starts[1] + 2 * part))]
    count_cross = remote(count_out, count_in, neighbour)
    second_out = [exchange(2, 0, HALF, cols, 2) for cols in parts]
    second_on = [forward(2, 0, HALF, cols) for cols in parts]
    third_early = exchange(3, 0, 32, every, 4)
    third_early_on = forward(3, 0, 32, every)
    third_out = [exchange(3, 32, 32, cols, 4) for cols in parts]
    third_on = [forward(3, 32, 32, cols) for cols in parts]
    pieces = [(0, every), (32, every), (16, parts[0]), (16, parts[1]), (48, parts[0]), (48, parts[1])]
    fourth_out = [exchange(4, start, 16, cols, 12) for start, cols in pieces]
    fourth_on = [forward(4, start, 16, cols) for start, cols in pieces]
    fourth_away = [forward(4, start, 16, cols, 4) for start, cols in pieces]
    fourth_over = [remote(block_part(4, start, 16, every), block_part(4, start + 16, 16, every), flip(me, 2))
                   for start in (0, 32)]
    later_out = {level: exchange(level, 0, HALF, every, 1 << (level - 1))
                 for level in range(5, levels + 1)}
    later_on = {level: forward(level, 0, HALF, every) for level in range(5, levels + 1)}

    def when_start(condition, copy):
        pl.when(condition)(copy.start)

    def set_seg():
        seg_load.wait()

        seg = seg_ref[...]
        first = jnp.sum(jnp.where(seg < 1, 1.0, 0.0), axis=1, keepdims=True)
        second = jnp.sum(jnp.where(seg < 2, 1.0, 0.0), axis=1, keepdims=True)
        spot = lax.broadcasted_iota(jnp.int32, (8, LANES), 0)
        count_out[...] = jnp.where(spot == 0, first, second)
        row = lax.broadcasted_iota(jnp.int32, (tokens, LANES), 0).astype(jnp.float32)
        lane = lax.broadcasted_iota(jnp.int32, (tokens, LANES), 1).astype(jnp.float32)
        row_seg = jnp.where(row >= first, 1.0, 0.0) + jnp.where(row >= second, 1.0, 0.0)
        kv[:, seg_columns] = jnp.where(lane == row_seg, -BIG, 0.0).astype(jnp.bfloat16)
        other = jnp.where(lane == row_seg, 0.0, jnp.where(lane < 4, 1.0, 0.0)).astype(jnp.bfloat16)
        query_seg[:tokens, :] = other
        query_seg[tokens:, :] = other

    for h, cols in enumerate(parts):
        if h == 1:
            set_seg()
        for one_load in loads[h]:
            one_load.wait()
        coarse[:, cols] = halve(kv[:, cols])
        sends[2][:, cols] = halve(coarse[:, cols])
        if h == 0:
            pl.semaphore_wait(barrier, len(masks) + jnp.where(middle, 1, 0) + jnp.where(has_cross, 1, 0))
        second_out[h].start()
    to_sibling.start()
    to_inner.start()
    when_start(has_cross, count_cross)
    sends[3][:32, :] = halve(sends[2][...])
    third_early.start()
    sends[4][:16, :] = halve(sends[3][:32, :])
    when_start(middle, fourth_out[0])

    @pl.when(jnp.logical_not(has_cross))
    def _():
        cross[...] = jnp.zeros(cross.shape, cross.dtype)
        spot = lax.broadcasted_iota(jnp.int32, (TILE, LANES), 1)
        cross[:, seg_columns] = jnp.where(spot == 3, -BIG, 0.0).astype(jnp.bfloat16)

    w_copy = pltpu.make_async_copy(w_hbm, w_vmem, w_sem)
    w_copy.start()
    q_load.wait()

    low_lanes = lax.broadcasted_iota(jnp.int32, (TILE, LANES), 1) < DH
    one = jnp.ones((TILE, LANES), jnp.bfloat16)
    zero = jnp.zeros((TILE, LANES), jnp.bfloat16)
    low_ones = jnp.where(low_lanes, one, zero)
    high_ones = jnp.where(low_lanes, zero, one)

    def columns(h, pair):
        at = starts[h] + (pair - h * (pairs // 2)) * LANES
        return (pl.ds(pl.multiple_of(at, LANES), LANES),
                pl.ds(pl.multiple_of(at + part, LANES), LANES))

    def score(left_side, spots, key_cols):
        right_side = jnp.concatenate(
            [jnp.concatenate([ref[base : base + TILE, key_cols], ref[base : base + TILE, seg_columns]],
                             axis=1) for ref, base in spots], axis=0)
        return lax.dot_general(left_side, right_side, (((1,), (1,)), ((), ())),
                               preferred_element_type=jnp.float32)

    def highest(scores):
        top = scores[:, :LANES]
        for at in range(LANES, scores.shape[1], LANES):
            top = jnp.maximum(top, scores[:, at : at + LANES])
        return jnp.broadcast_to(jnp.max(top, axis=1, keepdims=True), top.shape)

    def weigh(scores, top, spots, value_cols):
        half = top.shape[0] // 2
        left_side, right_side = [], []
        for index, (ref, base) in enumerate(spots):
            some = scores[:, index * LANES : (index + 1) * LANES]
            weights = jnp.exp(some - top).astype(jnp.bfloat16)
            values = ref[base : base + TILE, value_cols]
            left_side += [weights[:half], weights[half:]]
            right_side += [
                jnp.concatenate([jnp.where(low_lanes, values, zero), low_ones], axis=1),
                jnp.concatenate([jnp.where(low_lanes, zero, values), high_ones], axis=1),
            ]
        return jnp.dot(jnp.concatenate(left_side, axis=1), jnp.concatenate(right_side, axis=0),
                       preferred_element_type=jnp.float32)

    def rescale(old, top):
        shrink = jnp.exp(old - top)
        half = top.shape[0] // 2
        lanes = lax.broadcasted_iota(jnp.int32, (half, LANES), 1) < DH
        both = jnp.where(lanes, shrink[:half], shrink[half:])
        return jnp.concatenate([both, both], axis=1)

    def whole_step(h, pair, spots):
        key_cols, value_cols = columns(h, pair)
        left_side = jnp.concatenate([queries[pair], query_seg[...]], axis=1)
        scores = score(left_side, spots, key_cols)
        yield
        old = largest[pair]
        top = jnp.maximum(old, highest(scores))
        yield
        largest[pair] = top
        total[pair] = total[pair] * rescale(old, top) + weigh(scores, top, spots, value_cols)

    def last_step(h, pair, spots):
        key_cols, value_cols = columns(h, pair)
        left_side = jnp.concatenate([queries[pair], query_seg[...]], axis=1)
        scores = score(left_side, spots, key_cols)
        yield
        old = largest[pair]
        top = jnp.maximum(old, highest(scores))
        yield
        acc = total[pair] * rescale(old, top) + weigh(scores, top, spots, value_cols)
        context[:, pl.ds(pl.multiple_of(pair * LANES, LANES), LANES)] = (
            acc[:, :LANES] / acc[:, LANES:]).astype(jnp.bfloat16)

    def tile_step(h, pair, start, spots, last):
        key_cols, value_cols = columns(h, pair)
        heads = (pl.ds(start, TILE), pl.ds(pl.multiple_of(start + tokens, TILE), TILE))
        left_side = jnp.concatenate(
            [jnp.concatenate([queries[pair, head], query_seg[head, :]], axis=1) for head in heads], axis=0)
        scores = score(left_side, spots, key_cols)
        yield
        old = jnp.concatenate([largest[pair, head] for head in heads], axis=0)
        top = jnp.maximum(old, highest(scores))
        yield
        acc = total[pair, heads[0]] * rescale(old, top) + weigh(scores, top, spots, value_cols)
        if last:
            context[heads[0], pl.ds(pl.multiple_of(pair * LANES, LANES), LANES)] = (
                acc[:, :LANES] / acc[:, LANES:]).astype(jnp.bfloat16)
        else:
            for index, head in enumerate(heads):
                largest[pair, head] = top[index * TILE : (index + 1) * TILE]
            total[pair, heads[0]] = acc

    def run(steps):
        for _ in range(3):
            for step in steps:
                next(step, None)

    def halves(body):
        run([body(pair // (pairs // 2), pair) for pair in range(pairs)])

    near = [(kv, 0), (kv, TILE), (blocks[1], 0)]

    def first_step(h, pair):
        key_cols, value_cols = columns(h, pair)
        scaled = q_ref[:, pl.ds(pl.multiple_of(pair * LANES, LANES), LANES)] * jnp.bfloat16(DH**-0.5)
        lanes = lax.broadcasted_iota(jnp.int32, (tokens, LANES), 1) < DH
        none = jnp.zeros_like(scaled)
        both = jnp.concatenate([jnp.where(lanes, scaled, none), jnp.where(lanes, none, scaled)], axis=0)
        queries[pair] = both
        scores = score(jnp.concatenate([both, query_seg[...]], axis=1), near, key_cols)
        yield
        top = highest(scores)
        yield
        largest[pair] = top
        total[pair] = weigh(scores, top, near, value_cols)

    def relay(index, away=middle):
        @pl.when(middle)
        def _():
            fourth_out[index].wait_recv()
            fourth_on[index].start()

        @pl.when(away)
        def _():
            fourth_away[index].start()

    def outer_take(index):
        @pl.when(outer)
        def _():
            fourth_away[index].wait_recv()
            fourth_on[index].start()

        when_start(side, fourth_over[index])

    def side_take(*some):
        @pl.when(side)
        def _():
            for index in some:
                fourth_away[index].wait_recv()
                fourth_on[index].start()

    def span_of(h, body):
        run([body(h, pair) for pair in range(h * (pairs // 2), (h + 1) * (pairs // 2))])

    to_sibling.wait_recv()
    for h, cols in enumerate(parts):
        span_of(h, first_step)
        if h == 0:
            third_early.wait_recv()
            third_early_on.start()
            sends[4][32:48, :] = halve(blocks[3][pl.ds(mine, 32), :])
            when_start(middle, fourth_out[1])
        second_out[h].wait_recv()
        second_on[h].start()
        sends[3][32:, cols] = halve(blocks[2][pl.ds(mine, HALF), cols])
        third_out[h].start()
        sends[4][16:32, cols] = halve(sends[3][32:, cols])
        when_start(middle, fourth_out[2 + h])
        if h == 0:
            for copy in to_cross:
                when_start(near_cross, copy)
        relay(h)

    to_inner.wait_recv()
    halves(lambda h, pair: tile_step(h, pair, inner_row, [(inner, 0)], False))

    for copy in to_cross:
        when_start(soon_cross, copy)
    outer_take(0)
    for h, cols in enumerate(parts):
        third_out[h].wait_recv()
        third_on[h].start()
        sends[4][48:, cols] = halve(blocks[3][pl.ds(pl.multiple_of(mine + 32, 32), 32), cols])
        when_start(middle, fourth_out[4 + h])
        relay(2 + h, to_side)
        when_start(late_cross, to_cross[h])
        if h == 0:
            outer_take(1)

    @pl.when(has_cross)
    def _():
        count_cross.wait_recv()
        row = (lax.broadcasted_iota(jnp.int32, (TILE, LANES), 0) + inner_row).astype(jnp.float32)
        lane = lax.broadcasted_iota(jnp.int32, (TILE, LANES), 1).astype(jnp.float32)
        kind = jnp.where(row >= count_in[0:1, :], 1.0, 0.0) + jnp.where(row >= count_in[1:2, :], 1.0, 0.0)
        cross[:, seg_columns] = jnp.where(lane == kind, -BIG, 0.0).astype(jnp.bfloat16)

    for copy in second_on + [third_early_on] + third_on:
        copy.wait_recv()
    for h in range(2):
        span_of(h, lambda h, pair: whole_step(h, pair, [(blocks[2], 0), (blocks[3], 0)]))
        relay(4 + h, to_side)
        if h == 0:
            side_take(2)

    @pl.when(corner)
    def _():
        for index in range(2):
            fourth_over[index].wait_recv()
            fourth_on[2 + 2 * index].start()
            fourth_on[3 + 2 * index].start()

    side_take(3, 4, 5)

    for level in range(5, levels + 1):
        sends[level][:32, :] = halve(sends[level - 1][...])
        sends[level][32:, :] = halve(blocks[level - 1][pl.ds(mine, HALF), :])
        later_out[level].start()
        later_out[level].wait_recv()
        later_on[level].start()

    far = [(blocks[level], 0) for level in range(4, levels + 1)]

    @pl.when(middle)
    def _():
        for copy in fourth_on + list(later_on.values()):
            copy.wait_recv()
        halves(lambda h, pair: tile_step(h, pair, inner_row, far, True))
        for copy in to_cross:
            copy.wait_recv()
        halves(lambda h, pair: tile_step(h, pair, cross_row, far + [(cross, 0)], True))

    @pl.when(outer)
    def _():
        @pl.when(has_cross)
        def _():
            for copy in to_cross:
                copy.wait_recv()

        halves(lambda h, pair: tile_step(h, pair, cross_row, [(cross, 0)], False))
        for copy in fourth_on + list(later_on.values()):
            copy.wait_recv()
        halves(lambda h, pair: last_step(h, pair, far))

    w_copy.wait()

    @pl.loop(0, out_ref.shape[1] // 256, unroll=4)
    def _(block):
        cols = pl.ds(pl.multiple_of(block * 256, 256), 256)
        out_ref[:, cols] = jnp.dot(context[...], w_vmem[:, cols],
                                   preferred_element_type=jnp.float32).astype(jnp.bfloat16)

    for copy in [to_sibling, to_inner, third_early, third_early_on] + second_out + second_on + third_out + third_on:
        copy.wait_send()
    for copy in fourth_on + list(later_out.values()) + list(later_on.values()):
        copy.wait_send()

    @pl.when(middle)
    def _():
        for copy in fourth_out + fourth_away[:2]:
            copy.wait_send()

    @pl.when(to_side)
    def _():
        for copy in fourth_away[2:]:
            copy.wait_send()

    @pl.when(side)
    def _():
        for copy in fourth_over:
            copy.wait_send()

    @pl.when(has_cross)
    def _():
        for copy in to_cross + [count_cross]:
            copy.wait_send()


def on_device(devices, query_rows, key_rows, value_rows, segment_ids, out_weight):
    tokens, width = query_rows.shape
    levels = devices.bit_length() - 1
    span = 2 * width + LANES
    copies = 35 + 2 * (levels - 4)
    pairs = width // LANES
    bf16 = jnp.bfloat16
    scratch = [
        pltpu.VMEM((tokens, width), bf16),
        pltpu.VMEM((1, tokens), jnp.int32),
        pltpu.SemaphoreType.DMA((6,)),
        pltpu.VMEM((tokens, span), bf16),
        pltpu.VMEM((TILE, span), bf16),
        pltpu.VMEM((TILE, span), bf16),
        pltpu.VMEM((TILE, span), bf16),
        pltpu.VMEM((pairs, 2 * tokens, LANES), bf16),
        pltpu.VMEM((2 * tokens, LANES), bf16),
        pltpu.VMEM((pairs, 2 * tokens, LANES), jnp.float32),
        pltpu.VMEM((pairs, tokens, 2 * LANES), jnp.float32),
        pltpu.VMEM((tokens, width), bf16),
        pltpu.VMEM(out_weight.shape, bf16),
        pltpu.SemaphoreType.DMA,
        pltpu.SemaphoreType.DMA((copies,)),
        pltpu.SemaphoreType.DMA((copies,)),
        pltpu.VMEM((8, LANES), jnp.float32),
        pltpu.VMEM((8, LANES), jnp.float32),
    ]
    scratch += [pltpu.VMEM((HALF, span), bf16) for _ in range(2, levels + 1)]
    scratch += [pltpu.VMEM((TILE, span), bf16) for _ in range(1, levels + 1)]
    vmem = pl.BlockSpec(memory_space=pltpu.VMEM)
    return pl.pallas_call(
        functools.partial(attend, devices),
        out_shape=jax.ShapeDtypeStruct((tokens, width), bf16),
        in_specs=[pl.BlockSpec(memory_space=pltpu.HBM)] * 5,
        out_specs=vmem,
        scratch_shapes=scratch,
        compiler_params=pltpu.CompilerParams(
            collective_id=0, has_side_effects=True),
    )(query_rows, key_rows, value_rows, segment_ids.reshape(1, tokens), out_weight)


def solution(mesh):
    rows = P(("groups", "seq"), None)
    return jax.shard_map(
        functools.partial(on_device, mesh.shape["seq"]), mesh=mesh,
        in_specs=(rows, rows, rows, P(("groups", "seq")), P()),
        out_specs=rows, check_vma=False)
```

```python
import functools
import jax
import jax.numpy as jnp
from jax import lax
from jax.experimental import pallas as pl
from jax.experimental.pallas import tpu as pltpu
from jax.sharding import PartitionSpec as P

DH = 64
TILE = 128
LANES = 128
HALF = 64
BIG = 2.0**100
MESH = pl.DeviceIdType.MESH


def flip(index, mask):
    bit = 0
    while (1 << bit) <= mask:
        if mask & (1 << bit):
            index = index + (1 - 2 * ((index // (1 << bit)) % 2)) * (1 << bit)
        bit += 1
    return index


def halve(source):
    rows = source.shape[0]
    row = lax.broadcasted_iota(jnp.int32, (rows // 2, rows), 0)
    col = lax.broadcasted_iota(jnp.int32, (rows // 2, rows), 1)
    pick = jnp.where(col // 2 == row, 0.5, 0.0).astype(jnp.bfloat16)
    return jnp.dot(pick, source, preferred_element_type=jnp.float32).astype(jnp.bfloat16)


def attend(devices, q_hbm, k_hbm, v_hbm, seg_hbm, w_hbm, out_ref, q_ref, seg_ref, load_sem, kv, coarse, inner, cross,
           queries, query_seg, largest, total, context, w_vmem, w_sem, send_sem, recv_sem, count_out, count_in,
           out_vmem, out_sem, *rest):
    levels = devices.bit_length() - 1
    sends = dict(zip(range(2, levels + 1), rest))
    blocks = dict(zip(range(1, levels + 1), rest[levels - 1 :]))
    me = lax.axis_index("seq")
    core = me % 2
    tokens, width = q_hbm.shape
    pairs = width // LANES
    part = width // 2
    seg_at = 2 * part
    parts = (slice(0, 2 * part), slice(2 * part, 4 * part + LANES))
    starts = (0, 2 * part + LANES)
    every = slice(0, 4 * part + LANES)
    seg_columns = slice(seg_at, seg_at + LANES)

    middle = (me // 4 + me // 8) % 2 == 1
    outer = jnp.logical_not(middle)
    straight = (me // 2 + me // 4) % 2 == 0
    corner = jnp.logical_and(outer, straight)
    lag = middle
    side = jnp.logical_and(outer, jnp.logical_not(straight))
    to_side = jnp.logical_and(middle, straight)
    has_cross = jnp.logical_and(me + core > 0, me + core < devices)
    neighbour = me - 1 + 2 * core
    crooked = (me // 2 + core) % 2 == 0
    near_cross = jnp.logical_and(has_cross, jnp.logical_not(crooked))
    far_cross = jnp.logical_and(has_cross, crooked)
    soon_cross = jnp.logical_and(far_cross, jnp.logical_not(lag))
    late_cross = jnp.logical_and(far_cross, lag)
    inner_row = pl.multiple_of((1 - core) * TILE, TILE)
    cross_row = pl.multiple_of(core * TILE, TILE)
    mine = pl.multiple_of(core * HALF, HALF)

    barrier = pltpu.get_barrier_semaphore()
    masks = [1, 2, 4] + [1 << (level - 1) for level in range(5, levels + 1)]
    for mask in masks:
        pl.semaphore_signal(barrier, inc=1, device_id={"seq": flip(me, mask)}, device_id_type=MESH)

    @pl.when(middle)
    def _():
        pl.semaphore_signal(barrier, inc=1, device_id={"seq": flip(me, 12)}, device_id_type=MESH)

    @pl.when(has_cross)
    def _():
        pl.semaphore_signal(barrier, inc=1, device_id={"seq": neighbour}, device_id_type=MESH)

    def load(source, index, from_cols, to_cols):
        return pltpu.make_async_copy(source.at[:, from_cols], kv.at[:, to_cols], load_sem.at[index])

    seg_load = pltpu.make_async_copy(seg_hbm, seg_ref, load_sem.at[0])
    q_load = pltpu.make_async_copy(q_hbm, q_ref, load_sem.at[1])
    loads = []
    for h in range(2):
        base = starts[h]
        loads.append([
            load(k_hbm, 2 + 2 * h, slice(h * part, (h + 1) * part), slice(base, base + part)),
            load(v_hbm, 3 + 2 * h, slice(h * part, (h + 1) * part),
                 slice(base + part, base + 2 * part)),
        ])
    for some in loads:
        for one_load in some:
            one_load.start()
        if some is loads[0]:
            seg_load.start()
    q_load.start()
    made = []

    def remote(source, target, device):
        index = len(made)
        copy = pltpu.make_async_remote_copy(
            src_ref=source, dst_ref=target, send_sem=send_sem.at[index],
            recv_sem=recv_sem.at[index], device_id={"seq": device}, device_id_type=MESH)
        made.append(copy)
        return copy

    def block_part(level, start, rows, cols):
        return blocks[level].at[pl.ds(pl.multiple_of(mine + start, 16), rows), cols]

    def exchange(level, start, rows, cols, mask):
        return remote(sends[level].at[start : start + rows, cols],
                      block_part(level, start, rows, cols), flip(me, mask))

    def forward(level, start, rows, cols, mask=1):
        here = block_part(level, start, rows, cols)
        return remote(here, here, flip(me, mask))

    to_sibling = remote(coarse, blocks[1], flip(me, 1))
    to_inner = remote(kv.at[pl.ds(inner_row, TILE)], inner, flip(me, 1))
    to_cross = [remote(kv.at[pl.ds(cross_row, TILE), cols], cross.at[:, cols], neighbour)
                for cols in (parts[0], slice(starts[1], starts[1] + 2 * part))]
    count_cross = remote(count_out, count_in, neighbour)
    second_out = [exchange(2, 0, HALF, cols, 2) for cols in parts]
    second_on = [forward(2, 0, HALF, cols) for cols in parts]
    third_early = exchange(3, 0, 32, every, 4)
    third_early_on = forward(3, 0, 32, every)
    third_out = [exchange(3, 32, 32, cols, 4) for cols in parts]
    third_on = [forward(3, 32, 32, cols) for cols in parts]
    pieces = [(0, every), (32, every), (16, parts[0]), (16, parts[1]), (48, parts[0]), (48, parts[1])]
    fourth_out = [exchange(4, start, 16, cols, 12) for start, cols in pieces]
    fourth_on = [forward(4, start, 16, cols) for start, cols in pieces]
    fourth_away = [forward(4, start, 16, cols, 4) for start, cols in pieces]
    fourth_over = [remote(block_part(4, start, 16, every), block_part(4, start + 16, 16, every), flip(me, 2))
                   for start in (0, 32)]
    later_out = {level: exchange(level, 0, HALF, every, 1 << (level - 1))
                 for level in range(5, levels + 1)}
    later_on = {level: forward(level, 0, HALF, every) for level in range(5, levels + 1)}

    def when_start(condition, copy):
        pl.when(condition)(copy.start)

    def set_seg():
        seg_load.wait()

        seg = seg_ref[...]
        first = jnp.sum(jnp.where(seg < 1, 1.0, 0.0), axis=1, keepdims=True)
        second = jnp.sum(jnp.where(seg < 2, 1.0, 0.0), axis=1, keepdims=True)
        spot = lax.broadcasted_iota(jnp.int32, (8, LANES), 0)
        count_out[...] = jnp.where(spot == 0, first, second)
        row = lax.broadcasted_iota(jnp.int32, (tokens, LANES), 0).astype(jnp.float32)
        lane = lax.broadcasted_iota(jnp.int32, (tokens, LANES), 1).astype(jnp.float32)
        row_seg = jnp.where(row >= first, 1.0, 0.0) + jnp.where(row >= second, 1.0, 0.0)
        kv[:, seg_columns] = jnp.where(lane == row_seg, -BIG, 0.0).astype(jnp.bfloat16)
        other = jnp.where(lane == row_seg, 0.0, jnp.where(lane < 4, 1.0, 0.0)).astype(jnp.bfloat16)
        query_seg[:tokens, :] = other
        query_seg[tokens:, :] = other

    for h, cols in enumerate(parts):
        if h == 1:
            set_seg()
        for one_load in loads[h]:
            one_load.wait()
        coarse[:, cols] = halve(kv[:, cols])
        sends[2][:, cols] = halve(coarse[:, cols])
        if h == 0:
            pl.semaphore_wait(barrier, len(masks) + jnp.where(middle, 1, 0) + jnp.where(has_cross, 1, 0))
        second_out[h].start()
    to_sibling.start()
    to_inner.start()
    when_start(has_cross, count_cross)
    sends[3][:32, :] = halve(sends[2][...])
    third_early.start()
    sends[4][:16, :] = halve(sends[3][:32, :])
    when_start(middle, fourth_out[0])

    @pl.when(jnp.logical_not(has_cross))
    def _():
        cross[...] = jnp.zeros(cross.shape, cross.dtype)
        spot = lax.broadcasted_iota(jnp.int32, (TILE, LANES), 1)
        cross[:, seg_columns] = jnp.where(spot == 3, -BIG, 0.0).astype(jnp.bfloat16)

    w_copy = pltpu.make_async_copy(w_hbm, w_vmem, w_sem)
    w_copy.start()
    q_load.wait()

    low_lanes = lax.broadcasted_iota(jnp.int32, (TILE, LANES), 1) < DH
    one = jnp.ones((TILE, LANES), jnp.bfloat16)
    zero = jnp.zeros((TILE, LANES), jnp.bfloat16)
    low_ones = jnp.where(low_lanes, one, zero)
    high_ones = jnp.where(low_lanes, zero, one)

    def columns(h, pair):
        at = starts[h] + (pair - h * (pairs // 2)) * LANES
        return (pl.ds(pl.multiple_of(at, LANES), LANES),
                pl.ds(pl.multiple_of(at + part, LANES), LANES))

    def score(left_side, spots, key_cols):
        right_side = jnp.concatenate(
            [jnp.concatenate([ref[base : base + TILE, key_cols], ref[base : base + TILE, seg_columns]],
                             axis=1) for ref, base in spots], axis=0)
        return lax.dot_general(left_side, right_side, (((1,), (1,)), ((), ())),
                               preferred_element_type=jnp.float32)

    def highest(scores):
        top = scores[:, :LANES]
        for at in range(LANES, scores.shape[1], LANES):
            top = jnp.maximum(top, scores[:, at : at + LANES])
        return jnp.broadcast_to(jnp.max(top, axis=1, keepdims=True), top.shape)

    def weigh(scores, top, spots, value_cols):
        half = top.shape[0] // 2
        left_side, right_side = [], []
        for index, (ref, base) in enumerate(spots):
            some = scores[:, index * LANES : (index + 1) * LANES]
            weights = jnp.exp(some - top).astype(jnp.bfloat16)
            values = ref[base : base + TILE, value_cols]
            left_side += [weights[:half], weights[half:]]
            right_side += [
                jnp.concatenate([jnp.where(low_lanes, values, zero), low_ones], axis=1),
                jnp.concatenate([jnp.where(low_lanes, zero, values), high_ones], axis=1),
            ]
        return jnp.dot(jnp.concatenate(left_side, axis=1), jnp.concatenate(right_side, axis=0),
                       preferred_element_type=jnp.float32)

    def rescale(old, top):
        shrink = jnp.exp(old - top)
        half = top.shape[0] // 2
        lanes = lax.broadcasted_iota(jnp.int32, (half, LANES), 1) < DH
        both = jnp.where(lanes, shrink[:half], shrink[half:])
        return jnp.concatenate([both, both], axis=1)

    def whole_step(h, pair, spots):
        key_cols, value_cols = columns(h, pair)
        left_side = jnp.concatenate([queries[pair], query_seg[...]], axis=1)
        scores = score(left_side, spots, key_cols)
        yield
        old = largest[pair]
        top = jnp.maximum(old, highest(scores))
        yield
        largest[pair] = top
        total[pair] = total[pair] * rescale(old, top) + weigh(scores, top, spots, value_cols)

    def last_step(h, pair, spots):
        key_cols, value_cols = columns(h, pair)
        left_side = jnp.concatenate([queries[pair], query_seg[...]], axis=1)
        scores = score(left_side, spots, key_cols)
        yield
        old = largest[pair]
        top = jnp.maximum(old, highest(scores))
        yield
        acc = total[pair] * rescale(old, top) + weigh(scores, top, spots, value_cols)
        context[:, pl.ds(pl.multiple_of(pair * LANES, LANES), LANES)] = (
            acc[:, :LANES] / acc[:, LANES:]).astype(jnp.bfloat16)

    def tile_step(h, pair, start, spots, last):
        key_cols, value_cols = columns(h, pair)
        heads = (pl.ds(start, TILE), pl.ds(pl.multiple_of(start + tokens, TILE), TILE))
        left_side = jnp.concatenate(
            [jnp.concatenate([queries[pair, head], query_seg[head, :]], axis=1) for head in heads], axis=0)
        scores = score(left_side, spots, key_cols)
        yield
        old = jnp.concatenate([largest[pair, head] for head in heads], axis=0)
        top = jnp.maximum(old, highest(scores))
        yield
        acc = total[pair, heads[0]] * rescale(old, top) + weigh(scores, top, spots, value_cols)
        if last:
            context[heads[0], pl.ds(pl.multiple_of(pair * LANES, LANES), LANES)] = (
                acc[:, :LANES] / acc[:, LANES:]).astype(jnp.bfloat16)
        else:
            for index, head in enumerate(heads):
                largest[pair, head] = top[index * TILE : (index + 1) * TILE]
            total[pair, heads[0]] = acc

    def run(steps):
        for _ in range(3):
            for step in steps:
                next(step, None)

    def halves(body):
        run([body(pair // (pairs // 2), pair) for pair in range(pairs)])

    near = [(kv, 0), (kv, TILE), (blocks[1], 0)]

    def first_step(h, pair):
        key_cols, value_cols = columns(h, pair)
        scaled = q_ref[:, pl.ds(pl.multiple_of(pair * LANES, LANES), LANES)] * jnp.bfloat16(DH**-0.5)
        lanes = lax.broadcasted_iota(jnp.int32, (tokens, LANES), 1) < DH
        none = jnp.zeros_like(scaled)
        both = jnp.concatenate([jnp.where(lanes, scaled, none), jnp.where(lanes, none, scaled)], axis=0)
        queries[pair] = both
        scores = score(jnp.concatenate([both, query_seg[...]], axis=1), near, key_cols)
        yield
        top = highest(scores)
        yield
        largest[pair] = top
        total[pair] = weigh(scores, top, near, value_cols)

    def relay(index, away=middle):
        @pl.when(middle)
        def _():
            fourth_out[index].wait_recv()
            fourth_on[index].start()

        @pl.when(away)
        def _():
            fourth_away[index].start()

    def outer_take(index):
        @pl.when(outer)
        def _():
            fourth_away[index].wait_recv()
            fourth_on[index].start()

        when_start(side, fourth_over[index])

    def side_take(*some):
        @pl.when(side)
        def _():
            for index in some:
                fourth_away[index].wait_recv()
                fourth_on[index].start()

    def span_of(h, body):
        run([body(h, pair) for pair in range(h * (pairs // 2), (h + 1) * (pairs // 2))])

    to_sibling.wait_recv()
    for h, cols in enumerate(parts):
        span_of(h, first_step)
        if h == 0:
            third_early.wait_recv()
            third_early_on.start()
            sends[4][32:48, :] = halve(blocks[3][pl.ds(mine, 32), :])
            when_start(middle, fourth_out[1])
        second_out[h].wait_recv()
        second_on[h].start()
        sends[3][32:, cols] = halve(blocks[2][pl.ds(mine, HALF), cols])
        third_out[h].start()
        sends[4][16:32, cols] = halve(sends[3][32:, cols])
        when_start(middle, fourth_out[2 + h])
        if h == 0:
            for copy in to_cross:
                when_start(near_cross, copy)
        relay(h)

    to_inner.wait_recv()
    halves(lambda h, pair: tile_step(h, pair, inner_row, [(inner, 0)], False))

    for copy in to_cross:
        when_start(soon_cross, copy)
    outer_take(0)
    for h, cols in enumerate(parts):
        third_out[h].wait_recv()
        third_on[h].start()
        sends[4][48:, cols] = halve(blocks[3][pl.ds(pl.multiple_of(mine + 32, 32), 32), cols])
        when_start(middle, fourth_out[4 + h])
        relay(2 + h, to_side)
        when_start(late_cross, to_cross[h])
        if h == 0:
            outer_take(1)

    @pl.when(has_cross)
    def _():
        count_cross.wait_recv()
        row = (lax.broadcasted_iota(jnp.int32, (TILE, LANES), 0) + inner_row).astype(jnp.float32)
        lane = lax.broadcasted_iota(jnp.int32, (TILE, LANES), 1).astype(jnp.float32)
        kind = jnp.where(row >= count_in[0:1, :], 1.0, 0.0) + jnp.where(row >= count_in[1:2, :], 1.0, 0.0)
        cross[:, seg_columns] = jnp.where(lane == kind, -BIG, 0.0).astype(jnp.bfloat16)

    for copy in second_on + [third_early_on] + third_on:
        copy.wait_recv()
    for h in range(2):
        span_of(h, lambda h, pair: whole_step(h, pair, [(blocks[2], 0), (blocks[3], 0)]))
        relay(4 + h, to_side)
        if h == 0:
            side_take(2)

    @pl.when(corner)
    def _():
        for index in range(2):
            fourth_over[index].wait_recv()
            fourth_on[2 + 2 * index].start()
            fourth_on[3 + 2 * index].start()

    side_take(3, 4, 5)

    for level in range(5, levels + 1):
        sends[level][:32, :] = halve(sends[level - 1][...])
        sends[level][32:, :] = halve(blocks[level - 1][pl.ds(mine, HALF), :])
        later_out[level].start()
        later_out[level].wait_recv()
        later_on[level].start()

    far = [(blocks[level], 0) for level in range(4, levels + 1)]

    @pl.when(middle)
    def _():
        for copy in fourth_on + list(later_on.values()):
            copy.wait_recv()
        halves(lambda h, pair: tile_step(h, pair, inner_row, far, True))
        for copy in to_cross:
            copy.wait_recv()
        halves(lambda h, pair: tile_step(h, pair, cross_row, far + [(cross, 0)], True))

    @pl.when(outer)
    def _():
        @pl.when(has_cross)
        def _():
            for copy in to_cross:
                copy.wait_recv()

        halves(lambda h, pair: tile_step(h, pair, cross_row, [(cross, 0)], False))
        for copy in fourth_on + list(later_on.values()):
            copy.wait_recv()
        halves(lambda h, pair: last_step(h, pair, far))

    w_copy.wait()

    stores = []
    for block in range(width // 256):
        cols = slice(block * 256, (block + 1) * 256)
        out_vmem[:, cols] = jnp.dot(context[...], w_vmem[:, cols],
                                    preferred_element_type=jnp.float32).astype(jnp.bfloat16)
        store = pltpu.make_async_copy(out_vmem.at[:, cols], out_ref.at[:, cols], out_sem.at[block])
        store.start()
        stores.append(store)

    for copy in [to_sibling, to_inner, third_early, third_early_on] + second_out + second_on + third_out + third_on:
        copy.wait_send()
    for copy in fourth_on + list(later_out.values()) + list(later_on.values()):
        copy.wait_send()

    @pl.when(middle)
    def _():
        for copy in fourth_out + fourth_away[:2]:
            copy.wait_send()

    @pl.when(to_side)
    def _():
        for copy in fourth_away[2:]:
            copy.wait_send()

    @pl.when(side)
    def _():
        for copy in fourth_over:
            copy.wait_send()

    @pl.when(has_cross)
    def _():
        for copy in to_cross + [count_cross]:
            copy.wait_send()

    for store in stores:
        store.wait()


def on_device(devices, query_rows, key_rows, value_rows, segment_ids, out_weight):
    tokens, width = query_rows.shape
    levels = devices.bit_length() - 1
    span = 2 * width + LANES
    copies = 35 + 2 * (levels - 4)
    pairs = width // LANES
    bf16 = jnp.bfloat16
    scratch = [
        pltpu.VMEM((tokens, width), bf16),
        pltpu.VMEM((1, tokens), jnp.int32),
        pltpu.SemaphoreType.DMA((6,)),
        pltpu.VMEM((tokens, span), bf16),
        pltpu.VMEM((TILE, span), bf16),
        pltpu.VMEM((TILE, span), bf16),
        pltpu.VMEM((TILE, span), bf16),
        pltpu.VMEM((pairs, 2 * tokens, LANES), bf16),
        pltpu.VMEM((2 * tokens, LANES), bf16),
        pltpu.VMEM((pairs, 2 * tokens, LANES), jnp.float32),
        pltpu.VMEM((pairs, tokens, 2 * LANES), jnp.float32),
        pltpu.VMEM((tokens, width), bf16),
        pltpu.VMEM(out_weight.shape, bf16),
        pltpu.SemaphoreType.DMA,
        pltpu.SemaphoreType.DMA((copies,)),
        pltpu.SemaphoreType.DMA((copies,)),
        pltpu.VMEM((8, LANES), jnp.float32),
        pltpu.VMEM((8, LANES), jnp.float32),
        pltpu.VMEM((tokens, width), bf16),
        pltpu.SemaphoreType.DMA((width // 256,)),
    ]
    scratch += [pltpu.VMEM((HALF, span), bf16) for _ in range(2, levels + 1)]
    scratch += [pltpu.VMEM((TILE, span), bf16) for _ in range(1, levels + 1)]
    return pl.pallas_call(
        functools.partial(attend, devices),
        out_shape=jax.ShapeDtypeStruct((tokens, width), bf16),
        in_specs=[pl.BlockSpec(memory_space=pltpu.HBM)] * 5,
        out_specs=pl.BlockSpec(memory_space=pltpu.HBM),
        scratch_shapes=scratch,
        compiler_params=pltpu.CompilerParams(
            collective_id=0, has_side_effects=True),
    )(query_rows, key_rows, value_rows, segment_ids.reshape(1, tokens), out_weight)


def solution(mesh):
    rows = P(("groups", "seq"), None)
    return jax.shard_map(
        functools.partial(on_device, mesh.shape["seq"]), mesh=mesh,
        in_specs=(rows, rows, rows, P(("groups", "seq")), P()),
        out_specs=rows, check_vma=False)
```

```python
import functools
import jax
import jax.numpy as jnp
from jax import lax
from jax.experimental import pallas as pl
from jax.experimental.pallas import tpu as pltpu
from jax.sharding import PartitionSpec as P

DH = 64
TILE = 128
LANES = 128
HALF = 64
BIG = 2.0**100
MESH = pl.DeviceIdType.MESH


def flip(index, mask):
    bit = 0
    while (1 << bit) <= mask:
        if mask & (1 << bit):
            index = index + (1 - 2 * ((index // (1 << bit)) % 2)) * (1 << bit)
        bit += 1
    return index


def halve(source):
    rows = source.shape[0]
    row = lax.broadcasted_iota(jnp.int32, (rows // 2, rows), 0)
    col = lax.broadcasted_iota(jnp.int32, (rows // 2, rows), 1)
    pick = jnp.where(col // 2 == row, 0.5, 0.0).astype(jnp.bfloat16)
    return jnp.dot(pick, source, preferred_element_type=jnp.float32).astype(jnp.bfloat16)


def attend(devices, q_hbm, k_hbm, v_hbm, seg_hbm, w_hbm, out_ref, q_ref, seg_ref, load_sem, kv, coarse, inner, cross,
           queries, query_seg, largest, total, context, w_vmem, w_sem, send_sem, recv_sem, count_out, count_in,
           out_vmem, out_sem, *rest):
    levels = devices.bit_length() - 1
    sends = dict(zip(range(2, levels + 1), rest))
    blocks = dict(zip(range(1, levels + 1), rest[levels - 1 :]))
    me = lax.axis_index("seq")
    core = me % 2
    tokens, width = q_hbm.shape
    pairs = width // LANES
    part = width // 2
    seg_at = 2 * part
    parts = (slice(0, 2 * part), slice(2 * part, 4 * part + LANES))
    starts = (0, 2 * part + LANES)
    every = slice(0, 4 * part + LANES)
    seg_columns = slice(seg_at, seg_at + LANES)

    middle = (me // 4 + me // 8) % 2 == 1
    outer = jnp.logical_not(middle)
    straight = (me // 2 + me // 4) % 2 == 0
    corner = jnp.logical_and(outer, straight)
    lag = middle
    side = jnp.logical_and(outer, jnp.logical_not(straight))
    to_side = jnp.logical_and(middle, straight)
    has_cross = jnp.logical_and(me + core > 0, me + core < devices)
    neighbour = me - 1 + 2 * core
    crooked = (me // 2 + core) % 2 == 0
    near_cross = jnp.logical_and(has_cross, jnp.logical_not(crooked))
    far_cross = jnp.logical_and(has_cross, crooked)
    soon_cross = jnp.logical_and(far_cross, jnp.logical_not(lag))
    late_cross = jnp.logical_and(far_cross, lag)
    inner_row = pl.multiple_of((1 - core) * TILE, TILE)
    cross_row = pl.multiple_of(core * TILE, TILE)
    mine = pl.multiple_of(core * HALF, HALF)

    barrier = pltpu.get_barrier_semaphore()
    masks = [1, 2, 4] + [1 << (level - 1) for level in range(5, levels + 1)]
    for mask in masks:
        pl.semaphore_signal(barrier, inc=1, device_id={"seq": flip(me, mask)}, device_id_type=MESH)

    @pl.when(middle)
    def _():
        pl.semaphore_signal(barrier, inc=1, device_id={"seq": flip(me, 12)}, device_id_type=MESH)

    @pl.when(has_cross)
    def _():
        pl.semaphore_signal(barrier, inc=1, device_id={"seq": neighbour}, device_id_type=MESH)

    def load(source, index, from_cols, to_cols):
        return pltpu.make_async_copy(source.at[:, from_cols], kv.at[:, to_cols], load_sem.at[index])

    seg_load = pltpu.make_async_copy(seg_hbm, seg_ref, load_sem.at[0])
    q_load = pltpu.make_async_copy(q_hbm, q_ref, load_sem.at[1])
    loads = []
    for h in range(2):
        base = starts[h]
        loads.append([
            load(k_hbm, 2 + 2 * h, slice(h * part, (h + 1) * part), slice(base, base + part)),
            load(v_hbm, 3 + 2 * h, slice(h * part, (h + 1) * part),
                 slice(base + part, base + 2 * part)),
        ])
    for some in loads:
        for one_load in some:
            one_load.start()
        if some is loads[0]:
            seg_load.start()
    q_load.start()
    made = []

    def remote(source, target, device):
        index = len(made)
        copy = pltpu.make_async_remote_copy(
            src_ref=source, dst_ref=target, send_sem=send_sem.at[index],
            recv_sem=recv_sem.at[index], device_id={"seq": device}, device_id_type=MESH)
        made.append(copy)
        return copy

    def block_part(level, start, rows, cols):
        return blocks[level].at[pl.ds(pl.multiple_of(mine + start, 16), rows), cols]

    def exchange(level, start, rows, cols, mask):
        return remote(sends[level].at[start : start + rows, cols],
                      block_part(level, start, rows, cols), flip(me, mask))

    def forward(level, start, rows, cols, mask=1):
        here = block_part(level, start, rows, cols)
        return remote(here, here, flip(me, mask))

    to_sibling = remote(coarse, blocks[1], flip(me, 1))
    to_inner = remote(kv.at[pl.ds(inner_row, TILE)], inner, flip(me, 1))
    to_cross = [remote(kv.at[pl.ds(cross_row, TILE), cols], cross.at[:, cols], neighbour)
                for cols in (parts[0], slice(starts[1], starts[1] + 2 * part))]
    count_cross = remote(count_out, count_in, neighbour)
    second_out = [exchange(2, 0, HALF, cols, 2) for cols in parts]
    second_on = [forward(2, 0, HALF, cols) for cols in parts]
    third_early = exchange(3, 0, 32, every, 4)
    third_early_on = forward(3, 0, 32, every)
    third_out = [exchange(3, 32, 32, cols, 4) for cols in parts]
    third_on = [forward(3, 32, 32, cols) for cols in parts]
    pieces = [(0, every), (32, every), (16, parts[0]), (16, parts[1]), (48, parts[0]), (48, parts[1])]
    fourth_out = [exchange(4, start, 16, cols, 12) for start, cols in pieces]
    fourth_on = [forward(4, start, 16, cols) for start, cols in pieces]
    fourth_away = [forward(4, start, 16, cols, 4) for start, cols in pieces]
    fourth_over = [remote(block_part(4, start, 16, every), block_part(4, start + 16, 16, every), flip(me, 2))
                   for start in (0, 32)]
    later_out = {level: exchange(level, 0, HALF, every, 1 << (level - 1))
                 for level in range(5, levels + 1)}
    later_on = {level: forward(level, 0, HALF, every) for level in range(5, levels + 1)}

    def when_start(condition, copy):
        pl.when(condition)(copy.start)

    def set_seg():
        seg_load.wait()

        seg = seg_ref[...]
        first = jnp.sum(jnp.where(seg < 1, 1.0, 0.0), axis=1, keepdims=True)
        second = jnp.sum(jnp.where(seg < 2, 1.0, 0.0), axis=1, keepdims=True)
        spot = lax.broadcasted_iota(jnp.int32, (8, LANES), 0)
        count_out[...] = jnp.where(spot == 0, first, second)
        row = lax.broadcasted_iota(jnp.int32, (tokens, LANES), 0).astype(jnp.float32)
        lane = lax.broadcasted_iota(jnp.int32, (tokens, LANES), 1).astype(jnp.float32)
        row_seg = jnp.where(row >= first, 1.0, 0.0) + jnp.where(row >= second, 1.0, 0.0)
        kv[:, seg_columns] = jnp.where(lane == row_seg, -BIG, 0.0).astype(jnp.bfloat16)
        other = jnp.where(lane == row_seg, 0.0, jnp.where(lane < 4, 1.0, 0.0)).astype(jnp.bfloat16)
        query_seg[:tokens, :] = other
        query_seg[tokens:, :] = other

    for h, cols in enumerate(parts):
        if h == 1:
            set_seg()
        for one_load in loads[h]:
            one_load.wait()
        coarse[:, cols] = halve(kv[:, cols])
        sends[2][:, cols] = halve(coarse[:, cols])
        if h == 0:
            pl.semaphore_wait(barrier, len(masks) + jnp.where(middle, 1, 0) + jnp.where(has_cross, 1, 0))
        second_out[h].start()
    to_sibling.start()
    to_inner.start()
    when_start(has_cross, count_cross)
    sends[3][:32, :] = halve(sends[2][...])
    third_early.start()
    sends[4][:16, :] = halve(sends[3][:32, :])
    when_start(middle, fourth_out[0])

    @pl.when(jnp.logical_not(has_cross))
    def _():
        cross[...] = jnp.zeros(cross.shape, cross.dtype)
        spot = lax.broadcasted_iota(jnp.int32, (TILE, LANES), 1)
        cross[:, seg_columns] = jnp.where(spot == 3, -BIG, 0.0).astype(jnp.bfloat16)

    w_copy = pltpu.make_async_copy(w_hbm, w_vmem, w_sem)
    w_copy.start()
    q_load.wait()

    low_lanes = lax.broadcasted_iota(jnp.int32, (TILE, LANES), 1) < DH
    one = jnp.ones((TILE, LANES), jnp.bfloat16)
    zero = jnp.zeros((TILE, LANES), jnp.bfloat16)
    low_ones = jnp.where(low_lanes, one, zero)
    high_ones = jnp.where(low_lanes, zero, one)

    def columns(h, pair):
        at = starts[h] + (pair - h * (pairs // 2)) * LANES
        return (pl.ds(pl.multiple_of(at, LANES), LANES),
                pl.ds(pl.multiple_of(at + part, LANES), LANES))

    def score(left_side, spots, key_cols):
        right_side = jnp.concatenate(
            [jnp.concatenate([ref[base : base + TILE, key_cols], ref[base : base + TILE, seg_columns]],
                             axis=1) for ref, base in spots], axis=0)
        return lax.dot_general(left_side, right_side, (((1,), (1,)), ((), ())),
                               preferred_element_type=jnp.float32)

    def highest(scores):
        top = scores[:, :LANES]
        for at in range(LANES, scores.shape[1], LANES):
            top = jnp.maximum(top, scores[:, at : at + LANES])
        return jnp.broadcast_to(jnp.max(top, axis=1, keepdims=True), top.shape)

    def weigh(scores, top, spots, value_cols):
        half = top.shape[0] // 2
        left_side, right_side = [], []
        for index, (ref, base) in enumerate(spots):
            some = scores[:, index * LANES : (index + 1) * LANES]
            weights = jnp.exp(some - top).astype(jnp.bfloat16)
            values = ref[base : base + TILE, value_cols]
            left_side += [weights[:half], weights[half:]]
            right_side += [
                jnp.concatenate([jnp.where(low_lanes, values, zero), low_ones], axis=1),
                jnp.concatenate([jnp.where(low_lanes, zero, values), high_ones], axis=1),
            ]
        return jnp.dot(jnp.concatenate(left_side, axis=1), jnp.concatenate(right_side, axis=0),
                       preferred_element_type=jnp.float32)

    def rescale(old, top):
        shrink = jnp.exp(old - top)
        half = top.shape[0] // 2
        lanes = lax.broadcasted_iota(jnp.int32, (half, LANES), 1) < DH
        both = jnp.where(lanes, shrink[:half], shrink[half:])
        return jnp.concatenate([both, both], axis=1)

    def whole_step(h, pair, spots):
        key_cols, value_cols = columns(h, pair)
        left_side = jnp.concatenate([queries[pair], query_seg[...]], axis=1)
        scores = score(left_side, spots, key_cols)
        yield
        old = largest[pair]
        top = jnp.maximum(old, highest(scores))
        yield
        largest[pair] = top
        total[pair] = total[pair] * rescale(old, top) + weigh(scores, top, spots, value_cols)

    def last_step(h, pair, spots):
        key_cols, value_cols = columns(h, pair)
        left_side = jnp.concatenate([queries[pair], query_seg[...]], axis=1)
        scores = score(left_side, spots, key_cols)
        yield
        old = largest[pair]
        top = jnp.maximum(old, highest(scores))
        yield
        acc = total[pair] * rescale(old, top) + weigh(scores, top, spots, value_cols)
        context[:, pl.ds(pl.multiple_of(pair * LANES, LANES), LANES)] = (
            acc[:, :LANES] / acc[:, LANES:]).astype(jnp.bfloat16)

    def tile_step(h, pair, start, spots, last):
        key_cols, value_cols = columns(h, pair)
        heads = (pl.ds(start, TILE), pl.ds(pl.multiple_of(start + tokens, TILE), TILE))
        left_side = jnp.concatenate(
            [jnp.concatenate([queries[pair, head], query_seg[head, :]], axis=1) for head in heads], axis=0)
        scores = score(left_side, spots, key_cols)
        yield
        old = jnp.concatenate([largest[pair, head] for head in heads], axis=0)
        top = jnp.maximum(old, highest(scores))
        yield
        acc = total[pair, heads[0]] * rescale(old, top) + weigh(scores, top, spots, value_cols)
        if last:
            context[heads[0], pl.ds(pl.multiple_of(pair * LANES, LANES), LANES)] = (
                acc[:, :LANES] / acc[:, LANES:]).astype(jnp.bfloat16)
        else:
            for index, head in enumerate(heads):
                largest[pair, head] = top[index * TILE : (index + 1) * TILE]
            total[pair, heads[0]] = acc

    def run(steps):
        for _ in range(3):
            for step in steps:
                next(step, None)

    def halves(body):
        run([body(pair // (pairs // 2), pair) for pair in range(pairs)])

    near = [(kv, 0), (kv, TILE), (blocks[1], 0)]

    def first_step(h, pair):
        key_cols, value_cols = columns(h, pair)
        scaled = q_ref[:, pl.ds(pl.multiple_of(pair * LANES, LANES), LANES)] * jnp.bfloat16(DH**-0.5)
        lanes = lax.broadcasted_iota(jnp.int32, (tokens, LANES), 1) < DH
        none = jnp.zeros_like(scaled)
        both = jnp.concatenate([jnp.where(lanes, scaled, none), jnp.where(lanes, none, scaled)], axis=0)
        queries[pair] = both
        scores = score(jnp.concatenate([both, query_seg[...]], axis=1), near, key_cols)
        yield
        top = highest(scores)
        yield
        largest[pair] = top
        total[pair] = weigh(scores, top, near, value_cols)

    def relay(index, away=middle):
        @pl.when(middle)
        def _():
            fourth_out[index].wait_recv()
            fourth_on[index].start()

        @pl.when(away)
        def _():
            fourth_away[index].start()

    def outer_take(index):
        @pl.when(outer)
        def _():
            fourth_away[index].wait_recv()
            fourth_on[index].start()

        when_start(side, fourth_over[index])

    def side_take(*some):
        @pl.when(side)
        def _():
            for index in some:
                fourth_away[index].wait_recv()
                fourth_on[index].start()

    def span_of(h, body):
        run([body(h, pair) for pair in range(h * (pairs // 2), (h + 1) * (pairs // 2))])

    to_sibling.wait_recv()
    for h, cols in enumerate(parts):
        span_of(h, first_step)
        if h == 0:
            third_early.wait_recv()
            third_early_on.start()
            sends[4][32:48, :] = halve(blocks[3][pl.ds(mine, 32), :])
            when_start(middle, fourth_out[1])
        second_out[h].wait_recv()
        second_on[h].start()
        sends[3][32:, cols] = halve(blocks[2][pl.ds(mine, HALF), cols])
        third_out[h].start()
        sends[4][16:32, cols] = halve(sends[3][32:, cols])
        when_start(middle, fourth_out[2 + h])
        if h == 0:
            for copy in to_cross:
                when_start(near_cross, copy)
        relay(h)

    to_inner.wait_recv()
    halves(lambda h, pair: tile_step(h, pair, inner_row, [(inner, 0)], False))

    for copy in to_cross:
        when_start(soon_cross, copy)
    outer_take(0)
    for h, cols in enumerate(parts):
        third_out[h].wait_recv()
        third_on[h].start()
        sends[4][48:, cols] = halve(blocks[3][pl.ds(pl.multiple_of(mine + 32, 32), 32), cols])
        when_start(middle, fourth_out[4 + h])
        relay(2 + h, to_side)
        when_start(late_cross, to_cross[h])
        if h == 0:
            outer_take(1)

    @pl.when(has_cross)
    def _():
        count_cross.wait_recv()
        row = (lax.broadcasted_iota(jnp.int32, (TILE, LANES), 0) + inner_row).astype(jnp.float32)
        lane = lax.broadcasted_iota(jnp.int32, (TILE, LANES), 1).astype(jnp.float32)
        kind = jnp.where(row >= count_in[0:1, :], 1.0, 0.0) + jnp.where(row >= count_in[1:2, :], 1.0, 0.0)
        cross[:, seg_columns] = jnp.where(lane == kind, -BIG, 0.0).astype(jnp.bfloat16)

    for copy in second_on + [third_early_on] + third_on:
        copy.wait_recv()
    for h in range(2):
        span_of(h, lambda h, pair: whole_step(h, pair, [(blocks[2], 0), (blocks[3], 0)]))
        if h == 0:
            relay(4, to_side)
            relay(5, to_side)
        if h == 0:
            side_take(2)

    @pl.when(corner)
    def _():
        for index in range(2):
            fourth_over[index].wait_recv()
            fourth_on[2 + 2 * index].start()
            fourth_on[3 + 2 * index].start()

    side_take(3, 4, 5)

    for level in range(5, levels + 1):
        sends[level][:32, :] = halve(sends[level - 1][...])
        sends[level][32:, :] = halve(blocks[level - 1][pl.ds(mine, HALF), :])
        later_out[level].start()
        later_out[level].wait_recv()
        later_on[level].start()

    far = [(blocks[level], 0) for level in range(4, levels + 1)]

    @pl.when(middle)
    def _():
        for copy in fourth_on + list(later_on.values()):
            copy.wait_recv()
        halves(lambda h, pair: tile_step(h, pair, inner_row, far, True))
        for copy in to_cross:
            copy.wait_recv()
        halves(lambda h, pair: tile_step(h, pair, cross_row, far + [(cross, 0)], True))

    @pl.when(outer)
    def _():
        @pl.when(has_cross)
        def _():
            for copy in to_cross:
                copy.wait_recv()

        halves(lambda h, pair: tile_step(h, pair, cross_row, [(cross, 0)], False))
        for copy in fourth_on + list(later_on.values()):
            copy.wait_recv()
        halves(lambda h, pair: last_step(h, pair, far))

    w_copy.wait()

    stores = []
    for block in range(width // 256):
        cols = slice(block * 256, (block + 1) * 256)
        out_vmem[:, cols] = jnp.dot(context[...], w_vmem[:, cols],
                                    preferred_element_type=jnp.float32).astype(jnp.bfloat16)
        store = pltpu.make_async_copy(out_vmem.at[:, cols], out_ref.at[:, cols], out_sem.at[block])
        store.start()
        stores.append(store)

    for copy in [to_sibling, to_inner, third_early, third_early_on] + second_out + second_on + third_out + third_on:
        copy.wait_send()
    for copy in fourth_on + list(later_out.values()) + list(later_on.values()):
        copy.wait_send()

    @pl.when(middle)
    def _():
        for copy in fourth_out + fourth_away[:2]:
            copy.wait_send()

    @pl.when(to_side)
    def _():
        for copy in fourth_away[2:]:
            copy.wait_send()

    @pl.when(side)
    def _():
        for copy in fourth_over:
            copy.wait_send()

    @pl.when(has_cross)
    def _():
        for copy in to_cross + [count_cross]:
            copy.wait_send()

    for store in stores:
        store.wait()


def on_device(devices, query_rows, key_rows, value_rows, segment_ids, out_weight):
    tokens, width = query_rows.shape
    levels = devices.bit_length() - 1
    span = 2 * width + LANES
    copies = 35 + 2 * (levels - 4)
    pairs = width // LANES
    bf16 = jnp.bfloat16
    scratch = [
        pltpu.VMEM((tokens, width), bf16),
        pltpu.VMEM((1, tokens), jnp.int32),
        pltpu.SemaphoreType.DMA((6,)),
        pltpu.VMEM((tokens, span), bf16),
        pltpu.VMEM((TILE, span), bf16),
        pltpu.VMEM((TILE, span), bf16),
        pltpu.VMEM((TILE, span), bf16),
        pltpu.VMEM((pairs, 2 * tokens, LANES), bf16),
        pltpu.VMEM((2 * tokens, LANES), bf16),
        pltpu.VMEM((pairs, 2 * tokens, LANES), jnp.float32),
        pltpu.VMEM((pairs, tokens, 2 * LANES), jnp.float32),
        pltpu.VMEM((tokens, width), bf16),
        pltpu.VMEM(out_weight.shape, bf16),
        pltpu.SemaphoreType.DMA,
        pltpu.SemaphoreType.DMA((copies,)),
        pltpu.SemaphoreType.DMA((copies,)),
        pltpu.VMEM((8, LANES), jnp.float32),
        pltpu.VMEM((8, LANES), jnp.float32),
        pltpu.VMEM((tokens, width), bf16),
        pltpu.SemaphoreType.DMA((width // 256,)),
    ]
    scratch += [pltpu.VMEM((HALF, span), bf16) for _ in range(2, levels + 1)]
    scratch += [pltpu.VMEM((TILE, span), bf16) for _ in range(1, levels + 1)]
    return pl.pallas_call(
        functools.partial(attend, devices),
        out_shape=jax.ShapeDtypeStruct((tokens, width), bf16),
        in_specs=[pl.BlockSpec(memory_space=pltpu.HBM)] * 5,
        out_specs=pl.BlockSpec(memory_space=pltpu.HBM),
        scratch_shapes=scratch,
        compiler_params=pltpu.CompilerParams(
            collective_id=0, has_side_effects=True),
    )(query_rows, key_rows, value_rows, segment_ids.reshape(1, tokens), out_weight)


def solution(mesh):
    rows = P(("groups", "seq"), None)
    return jax.shard_map(
        functools.partial(on_device, mesh.shape["seq"]), mesh=mesh,
        in_specs=(rows, rows, rows, P(("groups", "seq")), P()),
        out_specs=rows, check_vma=False)
```
